32 devices in a mesh: ctx: 8 (over z, y), head: 4 (over x, core).
Axes of the slice: x: 2, y: 2, z: 4, core: 2. Of those that a mesh axis runs over, the one named last changes fastest.
Arguments:
- query_rows: bfloat16 [4096, 4096], P('ctx', 'head'), may hold values from -7.5 to 7.5
- key_rows: bfloat16 [4096, 4096], P('ctx', 'head'), may hold values from -7.5 to 7.5
- value_rows: bfloat16 [4096, 4096], P('ctx', 'head'), may hold values from -10 to 10
- centroids: float32 [32, 256, 128], P('head', 'ctx'), may hold values from -7.5 to 7.5
- norm_gain: float32 [4096], P('head'), may hold values from 0.1 to 1.9
- cluster_lists: int32 [32, 256, 32], P('head', 'ctx'), may hold values from 0 to 4095, as said below
- live_counts: int32 [32, 256, 8], P('head', 'ctx'), may hold values from 0 to 4, as said below
Outputs:
- normalized: bfloat16 [4096, 4096], P('ctx', 'head')
- swept_centroids: float32 [32, 256, 128], P('head', 'ctx')
- potentials: float32 [32, 256], P('head', 'ctx')
The draws below stay inside these ranges and needn't reach their ends.
Inputs may be any that keep to these rules, and one draw needn't show every extreme that they name: `cluster_lists`: for each head every token appears in exactly one live slot. Slots k * 4 to (k+1) * 4 - 1 of a list form segment k; its first live_counts[h, c, k] slots hold, in rising order, tokens of k * 512 to (k+1) * 512 - 1; the other slots hold 0. `live_counts`: for each head, each k and each g, the counts of clusters g * 32 to (g+1) * 32 - 1 in segment k sum to exactly 64. In every head some cluster has all its segments full.
All inputs are finite; a program needn't handle non-finite values.
Results may differ from the reference program's by a relative error of at most 0.012.
Values may be sent and summed in bfloat16 or wider, within the bound.
No kernel may reach another device: no remote copies, remote signals or barrier semaphores. Data moves between devices by JAX's collectives and lax.ppermute only.
A program may use at most 64 MiB of HBM per device.

```python
import math
import jax
import jax.numpy as jnp
from jax import lax

HEADS = 32
HD = 128
CLUSTERS = 256
ITERS = 5
TOK_DEV = 512
TOKENS = 4096
CL_DEV = 32
SEG = 4
BLOCK = 32
N_CTX = 8


def draw_query_rows(key, part):
    noise = jax.random.normal(jax.random.fold_in(key, 11), (TOKENS, HEADS, HD), jnp.float32)
    filled = noise
    return jnp.clip(filled, -7.5, 7.5).reshape(TOKENS, HEADS * HD).astype(jnp.bfloat16)


def draw_key_rows(key, part):
    noise = jax.random.normal(jax.random.fold_in(key, 21), (TOKENS, HEADS, HD), jnp.float32)
    filled = noise
    return jnp.clip(filled, -7.5, 7.5).reshape(TOKENS, HEADS * HD).astype(jnp.bfloat16)


def draw_centroids(key, part):
    noise = jax.random.normal(jax.random.fold_in(key, 31), (HEADS, CLUSTERS, HD), jnp.float32)
    filled = noise
    return jnp.clip(filled, -7.5, 7.5)


def draw_value_rows(key, part):
    ramp = jnp.arange(HEADS, dtype=jnp.float32) / max(HEADS - 1, 1)
    noise = jax.random.normal(jax.random.fold_in(key, 41), (TOKENS, HEADS, HD), jnp.float32)
    factor = 0.6 * jnp.power(3.0, ramp)
    filled = jnp.clip(noise * factor[None, :, None], -10.0, 10.0)
    return filled.reshape(TOKENS, HEADS * HD).astype(jnp.bfloat16)


def routing_tables(key):
    base = jax.random.fold_in(key, 4242)
    pair_dev = CL_DEV // 2
    order_scores = jax.random.randint(jax.random.fold_in(base, 1), (HEADS, N_CTX, CL_DEV), 0, 2 ** 16) * CL_DEV + jnp.arange(CL_DEV, dtype=jnp.int32)
    order = jnp.argsort(order_scores, axis=-1)
    inverse = jnp.argsort(order, axis=-1)
    centre = jax.random.randint(jax.random.fold_in(base, 2), (HEADS, N_CTX, pair_dev, 1), 0, SEG + 1)
    wobble = jax.random.randint(jax.random.fold_in(base, 3), (HEADS, N_CTX, pair_dev, N_CTX), -(SEG // 4), SEG // 4 + 1)
    first = jnp.clip(centre + wobble, 0, SEG)
    star = jax.random.randint(jax.random.fold_in(base, 4), (HEADS, 1, 1, 1), 0, N_CTX * pair_dev)
    pair_index = (jnp.arange(N_CTX, dtype=jnp.int32)[:, None] * pair_dev + jnp.arange(pair_dev, dtype=jnp.int32)[None, :])[None, :, :, None]
    first = jnp.where(pair_index == star, SEG, first)
    by_rank = jnp.stack([first, SEG - first], axis=3).reshape(HEADS, N_CTX, CL_DEV, N_CTX)
    by_cluster = jnp.take_along_axis(by_rank, jnp.broadcast_to(inverse[..., None], by_rank.shape), axis=2)
    counts = by_cluster.reshape(HEADS, CLUSTERS, N_CTX).astype(jnp.int32)
    per_source = counts.transpose(0, 2, 1)
    offsets = jnp.cumsum(per_source, axis=-1) - per_source
    slot_ids = jnp.arange(SEG, dtype=jnp.int32)
    position = offsets[..., None] + slot_ids
    is_live = slot_ids < per_source[..., None]
    shuffle_scores = jax.random.randint(jax.random.fold_in(base, 5), (HEADS, N_CTX, TOK_DEV), 0, 2 ** 12) * TOK_DEV + jnp.arange(TOK_DEV, dtype=jnp.int32)
    shuffle = jnp.argsort(shuffle_scores, axis=-1).astype(jnp.int32)
    clipped = jnp.clip(position, 0, TOK_DEV - 1).reshape(HEADS, N_CTX, CLUSTERS * SEG)
    picked = jnp.take_along_axis(shuffle, clipped, axis=-1).reshape(HEADS, N_CTX, CLUSTERS, SEG)
    ordered = jnp.sort(jnp.where(is_live, picked, TOK_DEV), axis=-1)
    source_start = (jnp.arange(N_CTX, dtype=jnp.int32) * TOK_DEV)[None, :, None, None]
    global_ids = jnp.where(is_live, ordered + source_start, 0)
    lists = global_ids.transpose(0, 2, 1, 3).reshape(HEADS, CLUSTERS, N_CTX * SEG)
    return (lists.astype(jnp.int32), counts)


def draw_cluster_lists(key, part):
    return routing_tables(key)[0]


def draw_live_counts(key, part):
    return routing_tables(key)[1]


def setup_inputs(seed: int = 0) -> dict:
    seeds = jax.random.split(jax.random.key(seed), 8)
    return {
        "query_rows": draw_query_rows(jax.random.fold_in(seeds[7], 71), 0),
        "key_rows": draw_key_rows(jax.random.fold_in(seeds[7], 71), 0),
        "value_rows": draw_value_rows(jax.random.fold_in(seeds[7], 71), 0),
        "centroids": draw_centroids(jax.random.fold_in(seeds[7], 71), 0),
        "norm_gain": jnp.clip(1.0 + 0.18 * jax.random.normal(seeds[4], (HEADS * HD,), jnp.float32), 0.1, 1.9),
        "cluster_lists": draw_cluster_lists(jax.random.fold_in(seeds[7], 71), 0),
        "live_counts": draw_live_counts(jax.random.fold_in(seeds[7], 71), 0),
    }


def balancing_head(keys_for_head, offset_begin):
    current = offset_begin
    potential = jnp.zeros((CLUSTERS,), jnp.float32)
    balance = math.log(TOKENS / CLUSTERS)
    for sweep_index in range(ITERS):
        rounded = current.astype(jnp.bfloat16)
        logits = jnp.dot(keys_for_head, rounded.T, preferred_element_type=jnp.float32) * HD ** (-0.5) + potential[None, :]
        row_peak = lax.optimization_barrier(jnp.max(logits, axis=-1, keepdims=True))
        log_total = row_peak + jnp.log(lax.optimization_barrier(jnp.sum(jnp.exp(logits - row_peak), axis=-1, keepdims=True)))
        logprob = logits - log_total
        column_peak = lax.optimization_barrier(jnp.max(logprob, axis=0))
        weights = jnp.exp(logprob - column_peak[None, :])
        mass_total = lax.optimization_barrier(jnp.sum(weights, axis=0))
        numerator = jnp.dot(weights.astype(jnp.bfloat16).T, keys_for_head, preferred_element_type=jnp.float32)
        current = numerator / mass_total[:, None]
        potential = potential + balance - (column_peak + jnp.log(mass_total))
    return (current, potential)

def reference(query_rows, key_rows, value_rows, centroids, norm_gain, cluster_lists, live_counts):
    head_ids = jnp.arange(HEADS, dtype=jnp.int32)

    def centroid_head(head_number):
        keys_for_head = lax.dynamic_slice_in_dim(key_rows, head_number * HD, HD, 1)
        return balancing_head(keys_for_head, centroids[head_number])
    swept_centroids, potentials = lax.map(centroid_head, head_ids)
    slot_ids = jnp.arange(BLOCK, dtype=jnp.int32)

    def attention_head(head_number):
        query_head = lax.dynamic_slice_in_dim(query_rows, head_number * HD, HD, 1)
        key_head = lax.dynamic_slice_in_dim(key_rows, head_number * HD, HD, 1)
        value_head = lax.dynamic_slice_in_dim(value_rows, head_number * HD, HD, 1)
        members = cluster_lists[head_number]
        seg_counts = live_counts[head_number]
        is_live = (slot_ids % SEG)[None, :] < jnp.repeat(seg_counts, SEG, axis=1)

        def one_block(block_item):
            block_members, block_live = block_item
            query_block = query_head[block_members]
            key_block = key_head[block_members]
            value_block = value_head[block_members]
            scores = jnp.dot(query_block, key_block.T, preferred_element_type=jnp.float32) * HD ** (-0.5)
            allowed = block_live[None, :] & (block_members[None, :] <= block_members[:, None])
            scores = jnp.where(allowed, scores, -1e+30)
            peak_row = lax.optimization_barrier(jnp.max(scores, axis=-1, keepdims=True))
            unnormed = jnp.exp(scores - peak_row)
            row_total = lax.optimization_barrier(jnp.sum(unnormed, axis=-1, keepdims=True))
            blended = jnp.dot(unnormed.astype(jnp.bfloat16), value_block, preferred_element_type=jnp.float32)
            return (blended / row_total).astype(jnp.bfloat16)
        block_out = lax.map(one_block, (members, is_live))
        target = jnp.where(is_live, members, TOKENS).reshape(-1)
        return jnp.zeros((TOKENS, HD), jnp.bfloat16).at[target].set(block_out.reshape(-1, HD), mode='drop')
    per_head = lax.map(attention_head, head_ids)
    attended = jnp.transpose(per_head, (1, 0, 2)).reshape(TOKENS, HEADS * HD)
    wide = attended.astype(jnp.float32)
    mean_square = lax.optimization_barrier(jnp.mean(wide * wide, axis=-1, keepdims=True))
    normalized = (wide * lax.rsqrt(mean_square + 1e-06) * norm_gain).astype(jnp.bfloat16)
    return (normalized, swept_centroids, potentials)
```

```python
import functools
import math

import jax
import jax.numpy as jnp
from jax import lax
from jax.experimental import pallas as pl
from jax.experimental.pallas import tpu as pltpu
from jax.sharding import PartitionSpec as P

ITERS = 5
LOG2E = math.log2(math.e)
TILE = 16
SMALLEST_MASS = 2.0**-80


def block_attention(block_item):
    block_rows, positions, is_live = block_item
    head_dim = block_rows.shape[1] // 3
    query_part = block_rows[:, :head_dim]
    key_part = block_rows[:, head_dim : 2 * head_dim]
    value_part = block_rows[:, 2 * head_dim :]
    scores = lax.dot_general(
        query_part, key_part, (((1,), (1,)), ((), ())), preferred_element_type=jnp.float32
    ) * head_dim ** (-0.5)
    allowed = is_live[None, :] & (positions[None, :] <= positions[:, None])
    scores = jnp.where(allowed, scores, -1e30)
    peak_row = jnp.max(scores, axis=-1, keepdims=True)
    unnormed = jnp.exp(scores - peak_row)
    row_total = jnp.sum(unnormed, axis=-1, keepdims=True)
    blended = jnp.dot(unnormed.astype(jnp.bfloat16), value_part, preferred_element_type=jnp.float32)
    return (blended / row_total).astype(jnp.bfloat16)


def attend_blocks(block_rows, cluster_lists, owned_live):
    count_blocks = block_rows.shape[0]
    positions = cluster_lists.reshape(count_blocks, -1)
    is_live = owned_live.reshape(count_blocks, -1)
    return lax.map(block_attention, (block_rows, positions, is_live))


def balancing_sweeps(per_head_keys, centroids, device_index, context_length):
    head_dev, cluster_dev, head_dim = centroids.shape
    clusters = cluster_dev * context_length
    tok_dev = per_head_keys.shape[0]
    balance = math.log(tok_dev * context_length / clusters)
    rounded = lax.all_gather(centroids.astype(jnp.bfloat16), "ctx", axis=1, tiled=True)
    potential = jnp.zeros((head_dev, clusters), jnp.float32)
    current_mine = centroids
    for sweep_index in range(ITERS):
        logits = (
            jnp.einsum("thd,hcd->thc", per_head_keys, rounded, preferred_element_type=jnp.float32)
            * head_dim ** (-0.5)
            + potential[None]
        )
        row_peak = jnp.max(logits, axis=-1, keepdims=True)
        log_total = row_peak + jnp.log(jnp.sum(jnp.exp(logits - row_peak), axis=-1, keepdims=True))
        logprob = logits - log_total
        column_peak = lax.pmax(jnp.max(logprob, axis=0), "ctx")
        weights = jnp.exp(logprob - column_peak[None])
        local_mass = jnp.sum(weights, axis=0)
        local_numerator = jnp.einsum(
            "thc,thd->hcd",
            weights.astype(jnp.bfloat16),
            per_head_keys,
            preferred_element_type=jnp.float32,
        )
        mass_total, numerator = lax.psum((local_mass, local_numerator), "ctx")
        current = numerator / mass_total[:, :, None]
        rounded = current.astype(jnp.bfloat16)
        current_mine = lax.dynamic_slice_in_dim(current, device_index * cluster_dev, cluster_dev, 1)
        potential = potential + balance - (column_peak + jnp.log(mass_total))
    return (
        current_mine,
        lax.dynamic_slice_in_dim(potential, device_index * cluster_dev, cluster_dev, 1),
    )


def local_wide(query_rows, key_rows, value_rows, centroids, norm_gain, cluster_lists, live_counts):
    context_length = lax.axis_size("ctx")
    device_index = lax.axis_index("ctx")
    tok_dev = query_rows.shape[0]
    head_dev, cluster_dev, head_dim = centroids.shape
    segment = cluster_lists.shape[2] // context_length
    query_heads = query_rows.reshape(tok_dev, head_dev, head_dim)
    per_head_keys = key_rows.reshape(tok_dev, head_dev, head_dim)
    value_heads = value_rows.reshape(tok_dev, head_dev, head_dim)
    swept_centroids, potentials = balancing_sweeps(
        per_head_keys, centroids, device_index, context_length
    )
    lists_split = cluster_lists.reshape(head_dev, cluster_dev, context_length, segment)
    asked_ids, asked_counts = (
        lax.all_to_all(lists_split, "ctx", split_axis=2, concat_axis=2, tiled=True),
        lax.all_to_all(live_counts, "ctx", split_axis=2, concat_axis=2, tiled=True),
    )
    slot_ids = jnp.arange(segment, dtype=jnp.int32)
    asked_live = slot_ids < asked_counts[..., None]
    local_ids = jnp.where(asked_live, asked_ids - device_index * tok_dev, 0)
    head_ids = jnp.broadcast_to(
        jnp.arange(head_dev, dtype=jnp.int32)[:, None, None, None], local_ids.shape
    )
    owned_live = slot_ids < live_counts[..., None]
    empty_out = jnp.zeros((tok_dev, head_dev, head_dim), jnp.bfloat16)
    sent_rows = jnp.concatenate(
        [
            query_heads[local_ids, head_ids],
            per_head_keys[local_ids, head_ids],
            value_heads[local_ids, head_ids],
        ],
        axis=-1,
    )
    arrived = lax.all_to_all(sent_rows, "ctx", split_axis=2, concat_axis=2, tiled=True)
    block_rows = arrived.reshape(head_dev * cluster_dev, context_length * segment, 3 * head_dim)
    block_out = attend_blocks(block_rows, cluster_lists, owned_live)
    returned = lax.all_to_all(
        block_out.reshape(head_dev, cluster_dev, context_length, segment, head_dim),
        "ctx",
        split_axis=2,
        concat_axis=2,
        tiled=True,
    )
    target = jnp.where(asked_live, local_ids, tok_dev)
    attended = empty_out.at[target, head_ids].set(returned, mode="drop")
    wide_attended = attended.reshape(tok_dev, head_dev * head_dim).astype(jnp.float32)
    squares = lax.psum(jnp.sum(wide_attended * wide_attended, axis=-1), "head")
    width = head_dev * head_dim * lax.axis_size("head")
    normalized = (wide_attended * lax.rsqrt(squares / width + 1e-06)[:, None] * norm_gain).astype(
        jnp.bfloat16
    )
    return (normalized, swept_centroids, potentials)


def sweeps_kernel(tile, key_ref, start_ref, out_ref, pot_ref, current, potential, logprob):
    tokens, head_dim = key_ref.shape
    clusters = start_ref.shape[0]
    tiles = tokens // tile
    scale = head_dim**-0.5 * LOG2E
    balance = math.log2(tokens / clusters)
    current[...] = start_ref[...].astype(jnp.float32)
    potential[...] = jnp.zeros_like(potential)

    def tile_logits(t, rounded, pot):
        keys = key_ref[pl.ds(pl.multiple_of(t * tile, tile), tile), :]
        dots = lax.dot_general(
            rounded, keys, (((1,), (1,)), ((), ())), preferred_element_type=jnp.float32
        )
        return dots * scale + pot, keys

    def sweep(_, carry):
        rounded = current[...].astype(jnp.bfloat16)
        pot = potential[...]

        def direct(t, sums):
            numerator, mass = sums
            logits, keys = tile_logits(t, rounded, pot)
            shifted = jnp.exp2(logits - jnp.max(logits, axis=0, keepdims=True))
            member = shifted * (1.0 / jnp.sum(shifted, axis=0, keepdims=True))
            numerator += jnp.dot(
                member.astype(jnp.bfloat16), keys, preferred_element_type=jnp.float32
            )
            for part in range(tile // 128):
                mass += member[:, part * 128 : (part + 1) * 128]
            return numerator, mass

        zeros = jnp.zeros((clusters, head_dim), jnp.float32)
        wide = jnp.zeros((clusters, 128), jnp.float32)
        numerator, mass = lax.fori_loop(0, tiles, direct, (zeros, wide))
        mass_total = jnp.sum(mass, axis=1, keepdims=True)
        current[...] = numerator / mass_total
        potential[...] = pot + balance - jnp.log2(mass_total)

        @pl.when(jnp.min(mass_total) < SMALLEST_MASS)
        def _():
            def peaks(t, peak):
                logits, _ = tile_logits(t, rounded, pot)
                row_peak = jnp.max(logits, axis=0, keepdims=True)
                total = jnp.sum(jnp.exp2(logits - row_peak), axis=0, keepdims=True)
                lp = logits - (row_peak + jnp.log2(total))
                logprob[t] = lp
                return jnp.maximum(peak, jnp.max(lp, axis=1, keepdims=True))

            lowest = jnp.full((clusters, 1), -jnp.inf, jnp.float32)
            peak = lax.fori_loop(0, tiles, peaks, lowest)

            def add(t, sums):
                numerator, mass = sums
                keys = key_ref[pl.ds(pl.multiple_of(t * tile, tile), tile), :]
                weights = jnp.exp2(logprob[t] - peak)
                numerator += jnp.dot(
                    weights.astype(jnp.bfloat16), keys, preferred_element_type=jnp.float32
                )
                return numerator, mass + jnp.sum(weights, axis=1, keepdims=True)

            column = jnp.zeros((clusters, 1), jnp.float32)
            numerator, mass_total = lax.fori_loop(0, tiles, add, (zeros, column))
            current[...] = numerator / mass_total
            potential[...] = pot + balance - (peak + jnp.log2(mass_total))

        return carry

    lax.fori_loop(0, ITERS, sweep, 0)
    out_ref[...] = current[...]
    pot_ref[...] = potential[...] * (1.0 / LOG2E)


def run_sweeps(keys, start, tile=256):
    tokens, head_dim = keys.shape
    clusters = start.shape[0]
    return pl.pallas_call(
        functools.partial(sweeps_kernel, tile),
        out_shape=(
            jax.ShapeDtypeStruct((clusters, head_dim), jnp.float32),
            jax.ShapeDtypeStruct((clusters, 1), jnp.float32),
        ),
        scratch_shapes=[
            pltpu.VMEM((clusters, head_dim), jnp.float32),
            pltpu.VMEM((clusters, 1), jnp.float32),
            pltpu.VMEM((tokens // tile, clusters, tile), jnp.float32),
        ],
        compiler_params=pltpu.CompilerParams(vmem_limit_bytes=32 * 2**20),
        cost_estimate=pl.CostEstimate(
            flops=4 * ITERS * tokens * clusters * head_dim,
            bytes_accessed=tokens * head_dim * 2,
            transcendentals=ITERS * tokens * clusters,
        ),
        name="sweeps",
    )(keys, start)


def attention_kernel(
    segment, q_ref, k_ref, v_ref, idx_col_ref, idx_row_ref, pos_col_ref, pos_row_ref, out_ref,
    gathered, blended,
):
    sources, tok_dev, head_dim = q_ref.shape
    slots = gathered.shape[2]
    chunk = idx_col_ref.shape[0]
    chunks = slots // chunk
    block = sources * TILE
    scale = head_dim**-0.5 * LOG2E

    def gather(step, carry):
        k, r = step // chunks, step % chunks
        column = pltpu.roll(idx_col_ref[...], 128 - step, 1)[:, :1]
        tokens = lax.broadcasted_iota(jnp.int32, (chunk, tok_dev), 1)
        picks = jnp.where(tokens == column, 1.0, 0.0).astype(jnp.bfloat16)
        rows = pl.ds(pl.multiple_of(r * chunk, chunk), chunk)
        for part, ref in enumerate((q_ref, k_ref, v_ref)):
            gathered[part, k, rows, :] = jnp.dot(
                picks, ref[k], preferred_element_type=jnp.float32
            ).astype(jnp.bfloat16)
        return carry

    lax.fori_loop(0, sources * chunks, gather, 0)

    row_cluster = lax.broadcasted_iota(jnp.int32, (block, block), 0) % TILE // segment
    col_cluster = lax.broadcasted_iota(jnp.int32, (block, block), 1) % TILE // segment
    same = row_cluster == col_cluster

    def attend(b, carry):
        rows = pl.ds(pl.multiple_of(b * TILE, TILE), TILE)
        query = gathered[0, :, rows, :].reshape(block, head_dim)
        key = gathered[1, :, rows, :].reshape(block, head_dim)
        value = gathered[2, :, rows, :].reshape(block, head_dim)
        scores = (
            lax.dot_general(
                query, key, (((1,), (1,)), ((), ())), preferred_element_type=jnp.float32
            )
            * scale
        )
        column = pltpu.roll(pos_col_ref[...], 128 - b, 1)[:, :1]
        row = pos_row_ref[pl.ds(b, 1), :]
        scores = jnp.where(same & (row <= column), scores, -1e30)
        unnormed = jnp.exp2(scores - jnp.max(scores, axis=1, keepdims=True))
        total = jnp.sum(unnormed, axis=1, keepdims=True)
        mixed = jnp.dot(unnormed.astype(jnp.bfloat16), value, preferred_element_type=jnp.float32)
        blended[:, rows, :] = (mixed / total).astype(jnp.bfloat16).reshape(sources, TILE, head_dim)
        return carry

    lax.fori_loop(0, slots // TILE, attend, 0)

    part_tokens = 128

    def scatter(step, carry):
        k, part = step // (tok_dev // part_tokens), step % (tok_dev // part_tokens)
        tokens = lax.broadcasted_iota(jnp.int32, (part_tokens, slots), 0) + part * part_tokens
        picks = jnp.where(tokens == idx_row_ref[pl.ds(k, 1), :], 1.0, 0.0).astype(jnp.bfloat16)
        rows = pl.ds(pl.multiple_of(part * part_tokens, part_tokens), part_tokens)
        out_ref[k, rows, :] = jnp.dot(
            picks, blended[k], preferred_element_type=jnp.float32
        ).astype(jnp.bfloat16)
        return carry

    lax.fori_loop(0, sources * tok_dev // part_tokens, scatter, 0)


def run_attention(query, key, value, lists):
    sources, tok_dev, head_dim = query.shape
    clusters, width = lists.shape
    segment = width // sources
    slots = clusters * segment
    blocks = slots // TILE
    chunk = 128
    by_segment = lists.reshape(clusters, sources, segment).transpose(1, 0, 2).reshape(sources, slots)
    idx_row = by_segment - (jnp.arange(sources, dtype=jnp.int32) * tok_dev)[:, None]
    idx_col = idx_row.reshape(-1, chunk).T
    pos = by_segment.reshape(sources, blocks, TILE).transpose(1, 0, 2).reshape(blocks, -1)
    pos_row = jnp.where(pos < 0, jnp.int32(2**30), pos)
    pos_col = pos.T
    widen = lambda a: jnp.pad(a, ((0, 0), (0, 128 - a.shape[1])))
    return pl.pallas_call(
        functools.partial(attention_kernel, segment),
        out_shape=jax.ShapeDtypeStruct(query.shape, jnp.bfloat16),
        scratch_shapes=[
            pltpu.VMEM((3, sources, slots, head_dim), jnp.bfloat16),
            pltpu.VMEM((sources, slots, head_dim), jnp.bfloat16),
        ],
        compiler_params=pltpu.CompilerParams(vmem_limit_bytes=48 * 2**20),
        cost_estimate=pl.CostEstimate(
            flops=2 * sources * slots * tok_dev * head_dim * 4,
            bytes_accessed=4 * sources * tok_dev * head_dim * 2,
            transcendentals=blocks * (sources * TILE) ** 2,
        ),
        name="attention",
    )(query, key, value, widen(idx_col), idx_row, widen(pos_col), pos_row)


def to_heads(rows, context_length):
    tok_dev, width = rows.shape
    split = rows.reshape(tok_dev, context_length, width // context_length).transpose(1, 0, 2)
    return lax.all_to_all(split, "ctx", split_axis=0, concat_axis=0, tiled=True)


def local(query_rows, key_rows, value_rows, centroids, norm_gain, cluster_lists, live_counts):
    context_length = lax.axis_size("ctx")
    tok_dev = query_rows.shape[0]
    head_dev, cluster_dev, head_dim = centroids.shape
    segment = cluster_lists.shape[2] // context_length
    if head_dev != context_length:
        return local_wide(
            query_rows, key_rows, value_rows, centroids, norm_gain, cluster_lists, live_counts
        )
    swap = functools.partial(
        lax.all_to_all, axis_name="ctx", split_axis=0, concat_axis=0, tiled=True
    )
    slot_ids = jnp.arange(segment, dtype=jnp.int32)
    live = slot_ids < live_counts[..., None]
    marked = jnp.where(live.reshape(cluster_lists.shape), cluster_lists, -1)
    lists = swap(marked).reshape(context_length * cluster_dev, -1)
    start = swap(centroids.astype(jnp.bfloat16)).reshape(-1, head_dim)
    keys = to_heads(key_rows, context_length)
    queries = to_heads(query_rows, context_length)
    values = to_heads(value_rows, context_length)
    swept, potential = run_sweeps(keys.reshape(-1, head_dim), start)
    swept_mine = swap(swept.reshape(context_length, cluster_dev, head_dim))
    potential_mine = swap(potential.reshape(context_length, cluster_dev))
    blended = run_attention(queries, keys, values, lists)
    attended = swap(blended).transpose(1, 0, 2).reshape(tok_dev, -1).astype(jnp.float32)
    squares = jnp.sum(attended * attended, axis=-1)
    for step in range(int(math.log2(lax.axis_size("head")))):
        ring = [(j, j ^ (1 << step)) for j in range(lax.axis_size("head"))]
        squares = squares + lax.ppermute(squares, "head", ring)
    width = head_dev * head_dim * lax.axis_size("head")
    normalized = (attended * lax.rsqrt(squares / width + 1e-06)[:, None] * norm_gain).astype(
        jnp.bfloat16
    )
    return (normalized, swept_mine, potential_mine)


def solution(mesh):
    placed = (
        P("ctx", "head"),
        P("ctx", "head"),
        P("ctx", "head"),
        P("head", "ctx", None),
        P("head"),
        P("head", "ctx", None),
        P("head", "ctx", None),
    )
    return jax.shard_map(
        local,
        mesh=mesh,
        in_specs=placed,
        out_specs=(P("ctx", "head"), P("head", "ctx", None), P("head", "ctx")),
        check_vma=False,
    )
```

```python
import functools
import math

import jax
import jax.numpy as jnp
from jax import lax
from jax.experimental import pallas as pl
from jax.experimental.pallas import tpu as pltpu
from jax.sharding import PartitionSpec as P

ITERS = 5
LOG2E = math.log2(math.e)
TILE = 16
DIGIT = 64
LANES = 128
SMALLEST_MASS = 2.0**-80
VMEM = pl.BlockSpec(memory_space=pltpu.VMEM)
SMEM = pl.BlockSpec(memory_space=pltpu.SMEM)
BY_ROWS = (((1,), (1,)), ((), ()))


def block_attention(block_item):
    block_rows, positions, is_live = block_item
    head_dim = block_rows.shape[1] // 3
    query_part = block_rows[:, :head_dim]
    key_part = block_rows[:, head_dim : 2 * head_dim]
    value_part = block_rows[:, 2 * head_dim :]
    scores = lax.dot_general(
        query_part, key_part, (((1,), (1,)), ((), ())), preferred_element_type=jnp.float32
    ) * head_dim ** (-0.5)
    allowed = is_live[None, :] & (positions[None, :] <= positions[:, None])
    scores = jnp.where(allowed, scores, -1e30)
    peak_row = jnp.max(scores, axis=-1, keepdims=True)
    unnormed = jnp.exp(scores - peak_row)
    row_total = jnp.sum(unnormed, axis=-1, keepdims=True)
    blended = jnp.dot(unnormed.astype(jnp.bfloat16), value_part, preferred_element_type=jnp.float32)
    return (blended / row_total).astype(jnp.bfloat16)


def attend_blocks(block_rows, cluster_lists, owned_live):
    count_blocks = block_rows.shape[0]
    positions = cluster_lists.reshape(count_blocks, -1)
    is_live = owned_live.reshape(count_blocks, -1)
    return lax.map(block_attention, (block_rows, positions, is_live))


def balancing_sweeps(per_head_keys, centroids, device_index, context_length):
    head_dev, cluster_dev, head_dim = centroids.shape
    clusters = cluster_dev * context_length
    tok_dev = per_head_keys.shape[0]
    balance = math.log(tok_dev * context_length / clusters)
    rounded = lax.all_gather(centroids.astype(jnp.bfloat16), "ctx", axis=1, tiled=True)
    potential = jnp.zeros((head_dev, clusters), jnp.float32)
    current_mine = centroids
    for _ in range(ITERS):
        logits = (
            jnp.einsum("thd,hcd->thc", per_head_keys, rounded, preferred_element_type=jnp.float32)
            * head_dim ** (-0.5)
            + potential[None]
        )
        row_peak = jnp.max(logits, axis=-1, keepdims=True)
        log_total = row_peak + jnp.log(jnp.sum(jnp.exp(logits - row_peak), axis=-1, keepdims=True))
        logprob = logits - log_total
        column_peak = lax.pmax(jnp.max(logprob, axis=0), "ctx")
        weights = jnp.exp(logprob - column_peak[None])
        local_mass = jnp.sum(weights, axis=0)
        local_numerator = jnp.einsum(
            "thc,thd->hcd",
            weights.astype(jnp.bfloat16),
            per_head_keys,
            preferred_element_type=jnp.float32,
        )
        mass_total, numerator = lax.psum((local_mass, local_numerator), "ctx")
        current = numerator / mass_total[:, :, None]
        rounded = current.astype(jnp.bfloat16)
        current_mine = lax.dynamic_slice_in_dim(current, device_index * cluster_dev, cluster_dev, 1)
        potential = potential + balance - (column_peak + jnp.log(mass_total))
    return (
        current_mine,
        lax.dynamic_slice_in_dim(potential, device_index * cluster_dev, cluster_dev, 1),
    )


def local_wide(query_rows, key_rows, value_rows, centroids, norm_gain, cluster_lists, live_counts):
    context_length = lax.axis_size("ctx")
    device_index = lax.axis_index("ctx")
    tok_dev = query_rows.shape[0]
    head_dev, cluster_dev, head_dim = centroids.shape
    segment = cluster_lists.shape[2] // context_length
    query_heads = query_rows.reshape(tok_dev, head_dev, head_dim)
    per_head_keys = key_rows.reshape(tok_dev, head_dev, head_dim)
    value_heads = value_rows.reshape(tok_dev, head_dev, head_dim)
    swept_centroids, potentials = balancing_sweeps(
        per_head_keys, centroids, device_index, context_length
    )
    lists_split = cluster_lists.reshape(head_dev, cluster_dev, context_length, segment)
    asked_ids, asked_counts = (
        lax.all_to_all(lists_split, "ctx", split_axis=2, concat_axis=2, tiled=True),
        lax.all_to_all(live_counts, "ctx", split_axis=2, concat_axis=2, tiled=True),
    )
    slot_ids = jnp.arange(segment, dtype=jnp.int32)
    asked_live = slot_ids < asked_counts[..., None]
    local_ids = jnp.where(asked_live, asked_ids - device_index * tok_dev, 0)
    head_ids = jnp.broadcast_to(
        jnp.arange(head_dev, dtype=jnp.int32)[:, None, None, None], local_ids.shape
    )
    owned_live = slot_ids < live_counts[..., None]
    empty_out = jnp.zeros((tok_dev, head_dev, head_dim), jnp.bfloat16)
    sent_rows = jnp.concatenate(
        [
            query_heads[local_ids, head_ids],
            per_head_keys[local_ids, head_ids],
            value_heads[local_ids, head_ids],
        ],
        axis=-1,
    )
    arrived = lax.all_to_all(sent_rows, "ctx", split_axis=2, concat_axis=2, tiled=True)
    block_rows = arrived.reshape(head_dev * cluster_dev, context_length * segment, 3 * head_dim)
    block_out = attend_blocks(block_rows, cluster_lists, owned_live)
    returned = lax.all_to_all(
        block_out.reshape(head_dev, cluster_dev, context_length, segment, head_dim),
        "ctx",
        split_axis=2,
        concat_axis=2,
        tiled=True,
    )
    target = jnp.where(asked_live, local_ids, tok_dev)
    attended = empty_out.at[target, head_ids].set(returned, mode="drop")
    wide_attended = attended.reshape(tok_dev, head_dev * head_dim).astype(jnp.float32)
    squares = lax.psum(jnp.sum(wide_attended * wide_attended, axis=-1), "head")
    width = head_dev * head_dim * lax.axis_size("head")
    normalized = (wide_attended * lax.rsqrt(squares / width + 1e-06)[:, None] * norm_gain).astype(
        jnp.bfloat16
    )
    return (normalized, swept_centroids, potentials)


def dot(a, b):
    return jnp.dot(a, b, preferred_element_type=jnp.float32)


def sweeps_kernel(tok_dev, cluster_dev, *refs):
    sources = (len(refs) - 4) // 2
    blocks, outs = refs[:sources], refs[sources : 2 * sources]
    keys, current, potential, scaled = refs[-4:]
    tokens, head_dim = keys.shape
    clusters = sources * cluster_dev
    scale = head_dim**-0.5 * LOG2E
    balance = math.log2(tokens / clusters)
    tile, wide = 2 * tok_dev, min(4, sources) * tok_dev
    for s, block in enumerate(blocks):
        keys[s * tok_dev : (s + 1) * tok_dev, :] = block[:tok_dev, :]
        current[s * cluster_dev : (s + 1) * cluster_dev, :] = block[
            tok_dev : tok_dev + cluster_dev, :
        ].astype(jnp.float32)
    potential[...] = jnp.zeros_like(potential)

    def part(t, size):
        return pl.ds(pl.multiple_of(t * size, size), size)

    def logits_of(t, rounded, pot):
        return (
            lax.dot_general(
                rounded, keys[part(t, tile), :], BY_ROWS, preferred_element_type=jnp.float32
            )
            * scale
            + pot
        )

    def fold(total, values, op):
        for p in range(values.shape[1] // LANES):
            total = op(total, values[:, p * LANES : (p + 1) * LANES])
        return total

    def sweep(_, carry):
        rounded = current[...].astype(jnp.bfloat16)
        pot = potential[...]
        flat = jnp.zeros((clusters, LANES), jnp.float32)

        def members(t, peak):
            logits = logits_of(t, rounded, pot)
            shifted = jnp.exp2(logits - jnp.max(logits, axis=0, keepdims=True))
            member = shifted * (1.0 / jnp.sum(shifted, axis=0, keepdims=True))
            scaled[:, part(t, tile)] = member
            return fold(peak, member, jnp.maximum)

        peak = jnp.max(
            lax.fori_loop(0, tokens // tile, members, flat), axis=1, keepdims=True
        )
        inverse = 1.0 / jnp.maximum(peak, SMALLEST_MASS)

        def add(t, sums):
            numerator, mass = sums
            weights = scaled[:, part(t, wide)] * inverse
            numerator += dot(weights.astype(jnp.bfloat16), keys[part(t, wide), :])
            return numerator, fold(mass, weights, jnp.add)

        sums = (jnp.zeros((clusters, head_dim), jnp.float32), flat)
        numerator, mass = lax.fori_loop(0, tokens // wide, add, sums)
        mass_total = jnp.sum(mass, axis=1, keepdims=True)
        current[...] = numerator / mass_total
        potential[...] = pot + balance - (jnp.log2(peak) + jnp.log2(mass_total))

        @pl.when(jnp.min(peak) < SMALLEST_MASS)
        def _():
            def peaks(t, top):
                logits = logits_of(t, rounded, pot)
                row_peak = jnp.max(logits, axis=0, keepdims=True)
                total = jnp.sum(jnp.exp2(logits - row_peak), axis=0, keepdims=True)
                logprob = logits - (row_peak + jnp.log2(total))
                scaled[:, part(t, tile)] = logprob
                return jnp.maximum(top, jnp.max(logprob, axis=1, keepdims=True))

            lowest = jnp.full((clusters, 1), -jnp.inf, jnp.float32)
            top = lax.fori_loop(0, tokens // tile, peaks, lowest)

            def again(t, sums):
                numerator, mass = sums
                weights = jnp.exp2(scaled[:, part(t, wide)] - top)
                numerator += dot(weights.astype(jnp.bfloat16), keys[part(t, wide), :])
                return numerator, mass + jnp.sum(weights, axis=1, keepdims=True)

            zeros = (jnp.zeros((clusters, head_dim), jnp.float32), jnp.zeros_like(lowest))
            numerator, mass_total = lax.fori_loop(0, tokens // wide, again, zeros)
            current[...] = numerator / mass_total
            potential[...] = pot + balance - (top + jnp.log2(mass_total))

        return carry

    lax.fori_loop(0, ITERS, sweep, 0)
    shape = (cluster_dev, LANES)
    diagonal = lax.broadcasted_iota(jnp.int32, shape, 0) == lax.broadcasted_iota(
        jnp.int32, shape, 1
    )
    for s in range(sources):
        rows = slice(s * cluster_dev, (s + 1) * cluster_dev)
        outs[s][:cluster_dev, :] = current[rows, :]
        column = jnp.broadcast_to(potential[rows, :] * (1.0 / LOG2E), shape)
        line = jnp.sum(jnp.where(diagonal, column, 0.0), axis=0, keepdims=True)
        outs[s][cluster_dev:, :] = jnp.broadcast_to(line, (8, LANES))


def run_sweeps(blocks, tok_dev, cluster_dev):
    sources, head_dim = len(blocks), blocks[0].shape[1]
    tokens, clusters = sources * tok_dev, sources * cluster_dev
    return pl.pallas_call(
        functools.partial(sweeps_kernel, tok_dev, cluster_dev),
        out_shape=[jax.ShapeDtypeStruct((cluster_dev + 8, head_dim), jnp.float32)] * sources,
        in_specs=[VMEM] * sources,
        out_specs=[VMEM] * sources,
        scratch_shapes=[
            pltpu.VMEM((tokens, head_dim), jnp.bfloat16),
            pltpu.VMEM((clusters, head_dim), jnp.float32),
            pltpu.VMEM((clusters, 1), jnp.float32),
            pltpu.VMEM((clusters, tokens), jnp.float32),
        ],
        compiler_params=pltpu.CompilerParams(vmem_limit_bytes=40 * 2**20),
        cost_estimate=pl.CostEstimate(
            flops=64 * ITERS * tokens * clusters * head_dim,
            bytes_accessed=tokens * head_dim * 2,
            transcendentals=ITERS * tokens * clusters,
        ),
        name="sweeps",
    )(*blocks)


def gather_rows(index, first, idx_col_ref, rows_in, out_ref):
    count, tok_dev, _ = rows_in.shape
    chunks = out_ref.shape[1] // LANES
    tokens = lax.broadcasted_iota(jnp.int32, (LANES, tok_dev), 1)

    def gather(s, carry):
        k = index ^ (s + first)
        table = pltpu.roll(idx_col_ref[...], LANES - k * chunks, 1)
        values = rows_in[s]
        for r in range(chunks):
            picks = jnp.where(tokens == table[:, r : r + 1], 1.0, 0.0).astype(jnp.bfloat16)
            out_ref[s, r * LANES : (r + 1) * LANES, :] = dot(picks, values).astype(jnp.bfloat16)
        return carry

    lax.fori_loop(0, count, gather, 0)


def position_features(index, rows_in, at):
    sources, tok_dev, _ = rows_in.shape
    shape = (tok_dev, LANES)
    token = lax.broadcasted_iota(jnp.int32, shape, 0)
    lane = lax.broadcasted_iota(jnp.int32, shape, 1)
    fine = token & (DIGIT - 1)
    for s in range(sources):
        coarse = (token + (index ^ s) * tok_dev) >> 6
        for number, columns in enumerate(
            ((1, 1, 1, coarse, fine), (coarse * DIGIT, fine, 1, -DIGIT, -1))
        ):
            feature = jnp.zeros(shape, jnp.int32)
            for place, column in enumerate(columns):
                feature = jnp.where(lane == place, column, feature)
            start = at + number * LANES
            rows_in[s, :, start : start + LANES] = feature.astype(jnp.float32).astype(jnp.bfloat16)


def gather_keys_kernel(index_ref, *refs):
    blocks, (idx_col_ref, out_ref, rows_in) = refs[:-3], refs[-3:]
    head_dim = blocks[0].shape[1]
    for s, ref in enumerate(blocks):
        rows_in[s, :, :head_dim] = ref[: rows_in.shape[1], :]
    position_features(index_ref[0], rows_in, head_dim)
    gather_rows(index_ref[0], 0, idx_col_ref, rows_in, out_ref)


def gather_near_kernel(index_ref, *refs):
    blocks, (idx_col_ref, out_ref, rows_in) = refs[:-3], refs[-3:]
    for s, ref in enumerate(blocks):
        rows_in[s] = ref[...]
    gather_rows(index_ref[0], 0, idx_col_ref, rows_in, out_ref)


def attention_kernel(segment, group, index_ref, after_ref, *refs):
    far = (len(refs) - 7) // 3
    sources = 2 * far
    blocks = refs[:far]
    near_ref, gk_ref, idx_col_ref, idx_row_ref = refs[far : far + 4]
    outs = refs[far + 4 : far + 4 + sources]
    rows_in, gathered, blended = refs[far + 4 + sources :]
    tok_dev, head_dim = rows_in.shape[1], outs[0].shape[1]
    slots = gk_ref.shape[1]
    block = sources * TILE
    scale = head_dim**-0.5 * LOG2E
    for s, ref in enumerate(blocks):
        rows_in[s] = ref[...]
    gather_rows(index_ref[0], far, idx_col_ref, rows_in, gathered)

    row_cluster = lax.broadcasted_iota(jnp.int32, (block, block), 0) % TILE // segment
    col_cluster = lax.broadcasted_iota(jnp.int32, (block, block), 1) % TILE // segment
    same = row_cluster == col_cluster
    flat = (block, head_dim)

    def attend(step, carry):
        rows = [
            pl.ds(pl.multiple_of((step * group + u) * TILE, TILE), TILE) for u in range(group)
        ]
        both = [jnp.concatenate([near_ref[:, r, :], gathered[:, r, :]], axis=0) for r in rows]
        keys = [gk_ref[:, r, :] for r in rows]

        def piece(values, number):
            at = number * head_dim
            return values[:, :, at : at + head_dim].reshape(flat)

        def against(left, right):
            return lax.dot_general(left, right, BY_ROWS, preferred_element_type=jnp.float32)

        ahead = [against(piece(k, 2), piece(k, 1)) for k in keys]
        scores = [
            jnp.where(
                same & (ahead[u] >= 1.0),
                against(piece(both[u], 0), piece(keys[u], 0)) * scale,
                -1e30,
            )
            for u in range(group)
        ]
        tops = [jnp.max(s, axis=1, keepdims=True) for s in scores]
        unnormed = [jnp.exp2(s - t) for s, t in zip(scores, tops)]
        totals = [jnp.sum(u, axis=1, keepdims=True) for u in unnormed]
        mixed = [
            dot(unnormed[u].astype(jnp.bfloat16), piece(both[u], 1))
            * (1.0 / totals[u])
            for u in range(group)
        ]
        for u in range(group):
            blended[:, rows[u], :] = (
                mixed[u].astype(jnp.bfloat16).reshape(sources, TILE, head_dim)
            )
        return carry

    lax.fori_loop(0, slots // TILE // group, attend, 0)

    tokens = lax.broadcasted_iota(jnp.int32, (tok_dev, slots), 0)
    for s in range(sources):
        wanted = idx_row_ref[pl.ds(index_ref[0] ^ s, 1), :]
        picks = jnp.where(tokens == wanted, 1.0, 0.0).astype(jnp.bfloat16)
        rows = dot(picks, blended[s]).astype(jnp.bfloat16)
        outs[s][:tok_dev, :] = rows
        wide = rows.astype(jnp.float32)
        squares = jnp.sum((wide * wide).T, axis=0, keepdims=True)
        lines = [squares[:, p : p + LANES] for p in range(0, tok_dev, LANES)]
        coarse = [line.astype(jnp.bfloat16).astype(jnp.float32) for line in lines]
        fine = [line - high for line, high in zip(lines, coarse)]
        spare = [jnp.zeros_like(lines[0])] * (TILE - 2 * len(lines))
        outs[s][tok_dev:, :] = jnp.concatenate(coarse + fine + spare, axis=0).astype(jnp.bfloat16)


def tables_kernel(tok_dev, segment, *refs):
    blocks, (idx_col_ref, idx_row_ref) = refs[:-2], refs[-2:]
    sources = len(blocks)
    width = sources * segment
    square = (LANES, LANES)
    row = lax.broadcasted_iota(jnp.int32, square, 0)
    lane = lax.broadcasted_iota(jnp.int32, square, 1)

    def ones_where(condition):
        return jnp.where(condition, 1.0, 0.0)

    spread = ones_where(row[:, :width] // segment == lane[:, :width]).astype(jnp.bfloat16)
    mine = (lane % segment == row % segment) & (lane < 2 * width)
    weight = jnp.where(row < width, float(DIGIT), 1.0) * ones_where(row < 2 * width)
    slot_of = row % width // segment
    columns = jnp.zeros(square, jnp.float32)
    by_row = (weight * ones_where(slot_of == lane))[:, :sources].T.astype(jnp.bfloat16)
    for r, block in enumerate(blocks):
        spread_digits = dot(spread, block[-width:, :])
        digits = jnp.where(mine, spread_digits, 0.0).astype(jnp.bfloat16)
        place = (lane // sources == slot_of) & (lane % sources == r)
        columns += dot(digits, (weight * ones_where(place)).astype(jnp.bfloat16))
        line = lax.dot_general(by_row, digits, BY_ROWS, preferred_element_type=jnp.float32)
        idx_row_ref[:, r * LANES : (r + 1) * LANES] = line.astype(jnp.int32) - tok_dev * row[:sources]
    idx_col_ref[...] = columns.astype(jnp.int32) - tok_dev * (lane // sources)


def run_tables(blocks, tok_dev, segment):
    sources = len(blocks)
    return pl.pallas_call(
        functools.partial(tables_kernel, tok_dev, segment),
        out_shape=(
            jax.ShapeDtypeStruct((LANES, LANES), jnp.int32),
            jax.ShapeDtypeStruct((sources, sources * LANES), jnp.int32),
        ),
        in_specs=[VMEM] * sources,
        out_specs=(VMEM, VMEM),
        compiler_params=pltpu.CompilerParams(vmem_limit_bytes=8 * 2**20),
        name="tables",
    )(*blocks)


def run_attention(index, after, key_blocks, pair_blocks, tables, tok_dev, segment, group=8):
    sources, head_dim = len(key_blocks), key_blocks[0].shape[1]
    idx_col, idx_row = tables
    slots = idx_row.shape[1]
    flops = 2 * sources * slots * tok_dev * head_dim
    gathered_keys = pl.pallas_call(
        gather_keys_kernel,
        out_shape=jax.ShapeDtypeStruct((sources, slots, 3 * head_dim), jnp.bfloat16),
        in_specs=[SMEM] + [VMEM] * (sources + 1),
        out_specs=VMEM,
        scratch_shapes=[pltpu.VMEM((sources, tok_dev, 3 * head_dim), jnp.bfloat16)],
        compiler_params=pltpu.CompilerParams(vmem_limit_bytes=24 * 2**20),
        cost_estimate=pl.CostEstimate(
            flops=4 * flops, bytes_accessed=6 * sources * tok_dev * head_dim, transcendentals=0
        ),
        name="gather_keys",
    )(index, *key_blocks, idx_col)
    near = sources // 2
    gathered_near = pl.pallas_call(
        gather_near_kernel,
        out_shape=jax.ShapeDtypeStruct((near, slots, 2 * head_dim), jnp.bfloat16),
        in_specs=[SMEM] + [VMEM] * (near + 1),
        out_specs=VMEM,
        scratch_shapes=[pltpu.VMEM((near, tok_dev, 2 * head_dim), jnp.bfloat16)],
        compiler_params=pltpu.CompilerParams(vmem_limit_bytes=24 * 2**20),
        cost_estimate=pl.CostEstimate(
            flops=4 * flops, bytes_accessed=6 * sources * tok_dev * head_dim, transcendentals=0
        ),
        name="gather_near",
    )(index, *pair_blocks[:near], idx_col)
    return pl.pallas_call(
        functools.partial(attention_kernel, segment, group),
        out_shape=[jax.ShapeDtypeStruct((tok_dev + TILE, head_dim), jnp.bfloat16)] * sources,
        in_specs=[SMEM, pl.BlockSpec(memory_space=pl.ANY)] + [VMEM] * (near + 4),
        out_specs=[VMEM] * sources,
        scratch_shapes=[
            pltpu.VMEM((near, tok_dev, 2 * head_dim), jnp.bfloat16),
            pltpu.VMEM((near, slots, 2 * head_dim), jnp.bfloat16),
            pltpu.VMEM((sources, slots, head_dim), jnp.bfloat16),
        ],
        compiler_params=pltpu.CompilerParams(vmem_limit_bytes=40 * 2**20),
        cost_estimate=pl.CostEstimate(
            flops=8 * flops,
            bytes_accessed=8 * sources * tok_dev * head_dim,
            transcendentals=slots // TILE * (sources * TILE) ** 2,
        ),
        name="attention",
    )(index, after, *pair_blocks[near:], gathered_near, gathered_keys, idx_col, idx_row)


def sum_squares_kernel(lines, *refs):
    total = sum(ref[-TILE:, :].astype(jnp.float32) for ref in refs[:-1])
    refs[-1][...] = total[:lines, :] + total[lines : 2 * lines, :]


def sum_squares(parts, tok_dev):
    lines = tok_dev // LANES
    return pl.pallas_call(
        functools.partial(sum_squares_kernel, lines),
        out_shape=jax.ShapeDtypeStruct((lines, LANES), jnp.float32),
        in_specs=[VMEM] * len(parts),
        out_specs=VMEM,
        compiler_params=pltpu.CompilerParams(vmem_limit_bytes=8 * 2**20),
        name="sum_squares",
    )(*parts)


def collect_kernel(index_ref, *refs):
    parts, (out_ref, pot_ref) = refs[:-2], refs[-2:]
    cluster_dev = out_ref.shape[1]
    for s, ref in enumerate(parts):
        head = index_ref[0] ^ s
        out_ref[head] = ref[:cluster_dev, :]
        pot_ref[pl.ds(head, 1), :] = ref[cluster_dev : cluster_dev + 1, :]


def collect(index, parts, cluster_dev):
    return pl.pallas_call(
        collect_kernel,
        out_shape=(
            jax.ShapeDtypeStruct((len(parts), cluster_dev, LANES), jnp.float32),
            jax.ShapeDtypeStruct((len(parts), LANES), jnp.float32),
        ),
        in_specs=[SMEM] + [VMEM] * len(parts),
        out_specs=(VMEM, VMEM),
        compiler_params=pltpu.CompilerParams(vmem_limit_bytes=8 * 2**20),
        name="collect",
    )(index, *parts)


def norm_kernel(width, heads, index_ref, *refs):
    parts, squares, (gain_ref, out_ref) = refs[:heads], refs[heads:-2], refs[-2:]
    head_dim = parts[0].shape[1]
    total = sum(ref[...] for ref in squares)
    inverse = lax.rsqrt(total / width + 1e-06)
    columns = [
        jnp.broadcast_to(inverse[p : p + 1, :], (LANES, LANES)).T for p in range(total.shape[0])
    ]
    for s, ref in enumerate(parts):
        head = index_ref[0] ^ s
        lanes = pl.ds(pl.multiple_of(head * head_dim, head_dim), head_dim)
        gain = gain_ref[:, lanes]
        for p, column in enumerate(columns):
            rows = slice(p * LANES, (p + 1) * LANES)
            out_ref[rows, lanes] = (ref[rows, :].astype(jnp.float32) * column * gain).astype(
                jnp.bfloat16
            )


def run_norm(index, parts, squares, gain, width, tok_dev):
    head_dim = parts[0].shape[1]
    return pl.pallas_call(
        functools.partial(norm_kernel, width, len(parts)),
        out_shape=jax.ShapeDtypeStruct((tok_dev, len(parts) * head_dim), jnp.bfloat16),
        in_specs=[SMEM] + [VMEM] * (len(parts) + len(squares) + 1),
        out_specs=VMEM,
        compiler_params=pltpu.CompilerParams(vmem_limit_bytes=24 * 2**20),
        name="norm",
    )(index, *parts, *squares, gain.reshape(1, -1))


def pack_kernel(index_ref, key_ref, centroid_ref, list_ref, count_ref, *outs):
    tok_dev = key_ref.shape[0]
    _, cluster_dev, head_dim = centroid_ref.shape
    width, sources = list_ref.shape[2], count_ref.shape[2]
    segment = width // sources
    owner = lax.broadcasted_iota(jnp.int32, (sources, width), 1) // segment
    spread = jnp.where(
        owner == lax.broadcasted_iota(jnp.int32, (sources, width), 0), 1.0, 0.0
    ).astype(jnp.bfloat16)
    slot = lax.broadcasted_iota(jnp.int32, (cluster_dev, width), 1) % segment
    at = lax.broadcasted_iota(jnp.int32, (width, head_dim), 1)
    source = lax.broadcasted_iota(jnp.int32, (width, head_dim), 0)
    first = jnp.where(at == source, 1.0, 0.0).astype(jnp.bfloat16)
    second = jnp.where(at == source + width, 1.0, 0.0).astype(jnp.bfloat16)
    for s, out in enumerate(outs):
        head = index_ref[0] ^ s
        lanes = pl.ds(pl.multiple_of(head * head_dim, head_dim), head_dim)
        out[:tok_dev, :] = key_ref[:, lanes]
        out[tok_dev : tok_dev + cluster_dev, :] = centroid_ref[head].astype(jnp.bfloat16)
        counts = dot(count_ref[head].astype(jnp.float32).astype(jnp.bfloat16), spread)
        marked = jnp.where(slot.astype(jnp.float32) < counts, list_ref[head], -TILE)
        coarse = (marked >> 6).astype(jnp.float32).astype(jnp.bfloat16)
        fine = (marked & (DIGIT - 1)).astype(jnp.float32).astype(jnp.bfloat16)
        out[tok_dev + cluster_dev :, :] = (dot(coarse, first) + dot(fine, second)).astype(
            jnp.bfloat16
        )


def pack_keys(index, key_rows, centroids, cluster_lists, live_counts):
    heads, cluster_dev, head_dim = centroids.shape
    rows = key_rows.shape[0] + 2 * cluster_dev
    return pl.pallas_call(
        pack_kernel,
        out_shape=[jax.ShapeDtypeStruct((rows, head_dim), jnp.bfloat16)] * heads,
        in_specs=[SMEM] + [VMEM] * 4,
        out_specs=[VMEM] * heads,
        compiler_params=pltpu.CompilerParams(vmem_limit_bytes=60 * 2**20),
        name="pack_keys",
    )(index, key_rows, centroids, cluster_lists, live_counts)


def shift_ring(size, step):
    return [(j, (j + step) % size) for j in range(size)]


def far_first(size):
    return list(range(size // 2, size)) + list(range(1, size // 2))


def pack_kernel(index_ref, key_ref, centroid_ref, list_ref, count_ref, *outs):
    tok_dev = key_ref.shape[0]
    _, cluster_dev, head_dim = centroid_ref.shape
    width, sources = list_ref.shape[2], count_ref.shape[2]
    segment = width // sources
    owner = lax.broadcasted_iota(jnp.int32, (sources, width), 1) // segment
    spread = jnp.where(
        owner == lax.broadcasted_iota(jnp.int32, (sources, width), 0), 1.0, 0.0
    ).astype(jnp.bfloat16)
    slot = lax.broadcasted_iota(jnp.int32, (cluster_dev, width), 1) % segment
    at = lax.broadcasted_iota(jnp.int32, (width, head_dim), 1)
    source = lax.broadcasted_iota(jnp.int32, (width, head_dim), 0)
    first = jnp.where(at == source, 1.0, 0.0).astype(jnp.bfloat16)
    second = jnp.where(at == source + width, 1.0, 0.0).astype(jnp.bfloat16)
    for s, out in enumerate(outs):
        head = index_ref[0] ^ s
        lanes = pl.ds(pl.multiple_of(head * head_dim, head_dim), head_dim)
        out[:tok_dev, :] = key_ref[:, lanes]
        out[tok_dev : tok_dev + cluster_dev, :] = centroid_ref[head].astype(jnp.bfloat16)
        counts = dot(count_ref[head].astype(jnp.float32).astype(jnp.bfloat16), spread)
        marked = jnp.where(slot.astype(jnp.float32) < counts, list_ref[head], -TILE)
        coarse = (marked >> 6).astype(jnp.float32).astype(jnp.bfloat16)
        fine = (marked & (DIGIT - 1)).astype(jnp.float32).astype(jnp.bfloat16)
        out[tok_dev + cluster_dev :, :] = (dot(coarse, first) + dot(fine, second)).astype(
            jnp.bfloat16
        )


def pack_keys(index, key_rows, centroids, cluster_lists, live_counts):
    heads, cluster_dev, head_dim = centroids.shape
    rows = key_rows.shape[0] + 2 * cluster_dev
    return pl.pallas_call(
        pack_kernel,
        out_shape=[jax.ShapeDtypeStruct((rows, head_dim), jnp.bfloat16)] * heads,
        in_specs=[SMEM] + [VMEM] * 4,
        out_specs=[VMEM] * heads,
        compiler_params=pltpu.CompilerParams(vmem_limit_bytes=60 * 2**20),
        name="pack_keys",
    )(index, key_rows, centroids, cluster_lists, live_counts)


def shift_ring(size, step):
    return [(j, (j + step) % size) for j in range(size)]


def exchange(blocks):
    size = len(blocks)
    arrived = list(blocks)
    for s in far_first(size):
        arrived[s] = lax.ppermute(blocks[s], "ctx", [(j, j ^ s) for j in range(size)])
    return arrived


def local(query_rows, key_rows, value_rows, centroids, norm_gain, cluster_lists, live_counts):
    context_length = lax.axis_size("ctx")
    head_dev = centroids.shape[0]
    if head_dev != context_length or context_length & (context_length - 1):
        return local_wide(
            query_rows, key_rows, value_rows, centroids, norm_gain, cluster_lists, live_counts
        )
    return local_heads(
        query_rows, key_rows, value_rows, centroids, norm_gain, cluster_lists, live_counts
    )


def local_heads(query_rows, key_rows, value_rows, centroids, norm_gain, cluster_lists, live_counts):
    context_length = lax.axis_size("ctx")
    head_size = lax.axis_size("head")
    tok_dev = query_rows.shape[0]
    head_dev, cluster_dev, head_dim = centroids.shape
    segment = cluster_lists.shape[2] // context_length
    index = lax.axis_index("ctx")
    place = index.astype(jnp.int32).reshape(1)

    def by_head(rows):
        return rows.reshape(tok_dev, head_dev, head_dim).transpose(1, 0, 2)

    pairs = jnp.concatenate([by_head(query_rows), by_head(value_rows)], axis=2)
    pairs = [
        lax.dynamic_index_in_dim(pairs, index ^ s, 0, keepdims=False)
        for s in range(context_length)
    ]
    key_blocks = exchange(pack_keys(place, key_rows, centroids, cluster_lists, live_counts))
    pair_blocks = exchange(pairs)
    tables = run_tables(key_blocks, tok_dev, segment)
    swept = run_sweeps(key_blocks, tok_dev, cluster_dev)
    outs = run_attention(place, swept[0], key_blocks, pair_blocks, tables, tok_dev, segment)
    parts = exchange(outs)
    swept_mine, potential_mine = collect(place, exchange(swept), cluster_dev)
    mine = sum_squares(parts, tok_dev)
    squares = [mine] + [
        lax.ppermute(mine, "head", shift_ring(head_size, step)) for step in range(1, head_size)
    ]
    features = head_dev * head_dim * head_size
    normalized = run_norm(place, parts, squares, norm_gain, features, tok_dev)
    return (normalized, swept_mine, potential_mine[:, :cluster_dev])


def solution(mesh):
    placed = (
        P("ctx", "head"),
        P("ctx", "head"),
        P("ctx", "head"),
        P("head", "ctx", None),
        P("head"),
        P("head", "ctx", None),
        P("head", "ctx", None),
    )
    return jax.shard_map(
        local,
        mesh=mesh,
        in_specs=placed,
        out_specs=(P("ctx", "head"), P("head", "ctx", None), P("head", "ctx")),
        check_vma=False,
    )
```

```python
import functools
import math

import jax
import jax.numpy as jnp
from jax import lax
from jax.experimental import pallas as pl
from jax.experimental.pallas import tpu as pltpu
from jax.sharding import PartitionSpec as P

ITERS = 5
LOG2E = math.log2(math.e)
TILE = 16
DIGIT = 64
LANES = 128
SMALLEST_MASS = 2.0**-80
VMEM = pl.BlockSpec(memory_space=pltpu.VMEM)
SMEM = pl.BlockSpec(memory_space=pltpu.SMEM)
BY_ROWS = (((1,), (1,)), ((), ()))


def block_attention(block_item):
    block_rows, positions, is_live = block_item
    head_dim = block_rows.shape[1] // 3
    query_part = block_rows[:, :head_dim]
    key_part = block_rows[:, head_dim : 2 * head_dim]
    value_part = block_rows[:, 2 * head_dim :]
    scores = lax.dot_general(
        query_part, key_part, (((1,), (1,)), ((), ())), preferred_element_type=jnp.float32
    ) * head_dim ** (-0.5)
    allowed = is_live[None, :] & (positions[None, :] <= positions[:, None])
    scores = jnp.where(allowed, scores, -1e30)
    peak_row = jnp.max(scores, axis=-1, keepdims=True)
    unnormed = jnp.exp(scores - peak_row)
    row_total = jnp.sum(unnormed, axis=-1, keepdims=True)
    blended = jnp.dot(unnormed.astype(jnp.bfloat16), value_part, preferred_element_type=jnp.float32)
    return (blended / row_total).astype(jnp.bfloat16)


def attend_blocks(block_rows, cluster_lists, owned_live):
    count_blocks = block_rows.shape[0]
    positions = cluster_lists.reshape(count_blocks, -1)
    is_live = owned_live.reshape(count_blocks, -1)
    return lax.map(block_attention, (block_rows, positions, is_live))


def balancing_sweeps(per_head_keys, centroids, device_index, context_length):
    head_dev, cluster_dev, head_dim = centroids.shape
    clusters = cluster_dev * context_length
    tok_dev = per_head_keys.shape[0]
    balance = math.log(tok_dev * context_length / clusters)
    rounded = lax.all_gather(centroids.astype(jnp.bfloat16), "ctx", axis=1, tiled=True)
    potential = jnp.zeros((head_dev, clusters), jnp.float32)
    current_mine = centroids
    for _ in range(ITERS):
        logits = (
            jnp.einsum("thd,hcd->thc", per_head_keys, rounded, preferred_element_type=jnp.float32)
            * head_dim ** (-0.5)
            + potential[None]
        )
        row_peak = jnp.max(logits, axis=-1, keepdims=True)
        log_total = row_peak + jnp.log(jnp.sum(jnp.exp(logits - row_peak), axis=-1, keepdims=True))
        logprob = logits - log_total
        column_peak = lax.pmax(jnp.max(logprob, axis=0), "ctx")
        weights = jnp.exp(logprob - column_peak[None])
        local_mass = jnp.sum(weights, axis=0)
        local_numerator = jnp.einsum(
            "thc,thd->hcd",
            weights.astype(jnp.bfloat16),
            per_head_keys,
            preferred_element_type=jnp.float32,
        )
        mass_total, numerator = lax.psum((local_mass, local_numerator), "ctx")
        current = numerator / mass_total[:, :, None]
        rounded = current.astype(jnp.bfloat16)
        current_mine = lax.dynamic_slice_in_dim(current, device_index * cluster_dev, cluster_dev, 1)
        potential = potential + balance - (column_peak + jnp.log(mass_total))
    return (
        current_mine,
        lax.dynamic_slice_in_dim(potential, device_index * cluster_dev, cluster_dev, 1),
    )


def local_wide(query_rows, key_rows, value_rows, centroids, norm_gain, cluster_lists, live_counts):
    context_length = lax.axis_size("ctx")
    device_index = lax.axis_index("ctx")
    tok_dev = query_rows.shape[0]
    head_dev, cluster_dev, head_dim = centroids.shape
    segment = cluster_lists.shape[2] // context_length
    query_heads = query_rows.reshape(tok_dev, head_dev, head_dim)
    per_head_keys = key_rows.reshape(tok_dev, head_dev, head_dim)
    value_heads = value_rows.reshape(tok_dev, head_dev, head_dim)
    swept_centroids, potentials = balancing_sweeps(
        per_head_keys, centroids, device_index, context_length
    )
    lists_split = cluster_lists.reshape(head_dev, cluster_dev, context_length, segment)
    asked_ids, asked_counts = (
        lax.all_to_all(lists_split, "ctx", split_axis=2, concat_axis=2, tiled=True),
        lax.all_to_all(live_counts, "ctx", split_axis=2, concat_axis=2, tiled=True),
    )
    slot_ids = jnp.arange(segment, dtype=jnp.int32)
    asked_live = slot_ids < asked_counts[..., None]
    local_ids = jnp.where(asked_live, asked_ids - device_index * tok_dev, 0)
    head_ids = jnp.broadcast_to(
        jnp.arange(head_dev, dtype=jnp.int32)[:, None, None, None], local_ids.shape
    )
    owned_live = slot_ids < live_counts[..., None]
    empty_out = jnp.zeros((tok_dev, head_dev, head_dim), jnp.bfloat16)
    sent_rows = jnp.concatenate(
        [
            query_heads[local_ids, head_ids],
            per_head_keys[local_ids, head_ids],
            value_heads[local_ids, head_ids],
        ],
        axis=-1,
    )
    arrived = lax.all_to_all(sent_rows, "ctx", split_axis=2, concat_axis=2, tiled=True)
    block_rows = arrived.reshape(head_dev * cluster_dev, context_length * segment, 3 * head_dim)
    block_out = attend_blocks(block_rows, cluster_lists, owned_live)
    returned = lax.all_to_all(
        block_out.reshape(head_dev, cluster_dev, context_length, segment, head_dim),
        "ctx",
        split_axis=2,
        concat_axis=2,
        tiled=True,
    )
    target = jnp.where(asked_live, local_ids, tok_dev)
    attended = empty_out.at[target, head_ids].set(returned, mode="drop")
    wide_attended = attended.reshape(tok_dev, head_dev * head_dim).astype(jnp.float32)
    squares = lax.psum(jnp.sum(wide_attended * wide_attended, axis=-1), "head")
    width = head_dev * head_dim * lax.axis_size("head")
    normalized = (wide_attended * lax.rsqrt(squares / width + 1e-06)[:, None] * norm_gain).astype(
        jnp.bfloat16
    )
    return (normalized, swept_centroids, potentials)


def dot(a, b):
    return jnp.dot(a, b, preferred_element_type=jnp.float32)


def sweeps_kernel(tok_dev, cluster_dev, *refs):
    sources = (len(refs) - 4) // 2
    blocks, outs = refs[:sources], refs[sources : 2 * sources]
    keys, current, potential, scaled = refs[-4:]
    tokens, head_dim = keys.shape
    clusters = sources * cluster_dev
    scale = head_dim**-0.5 * LOG2E
    balance = math.log2(tokens / clusters)
    tile, wide = 2 * tok_dev, min(4, sources) * tok_dev
    for s, block in enumerate(blocks):
        keys[s * tok_dev : (s + 1) * tok_dev, :] = block[:tok_dev, :]
        current[s * cluster_dev : (s + 1) * cluster_dev, :] = block[
            tok_dev : tok_dev + cluster_dev, :
        ].astype(jnp.float32)
    potential[...] = jnp.zeros_like(potential)

    def part(t, size):
        return pl.ds(pl.multiple_of(t * size, size), size)

    def logits_of(t, rounded, pot):
        return (
            lax.dot_general(
                rounded, keys[part(t, tile), :], BY_ROWS, preferred_element_type=jnp.float32
            )
            * scale
            + pot
        )

    def fold(total, values, op):
        for p in range(values.shape[1] // LANES):
            total = op(total, values[:, p * LANES : (p + 1) * LANES])
        return total

    def sweep(_, carry):
        rounded = current[...].astype(jnp.bfloat16)
        pot = potential[...]
        flat = jnp.zeros((clusters, LANES), jnp.float32)

        def members(t, peak):
            logits = logits_of(t, rounded, pot)
            shifted = jnp.exp2(logits - jnp.max(logits, axis=0, keepdims=True))
            member = shifted * (1.0 / jnp.sum(shifted, axis=0, keepdims=True))
            scaled[:, part(t, tile)] = member
            return fold(peak, member, jnp.maximum)

        peak = jnp.max(
            lax.fori_loop(0, tokens // tile, members, flat), axis=1, keepdims=True
        )
        inverse = 1.0 / jnp.maximum(peak, SMALLEST_MASS)

        def add(t, sums):
            numerator, mass = sums
            weights = scaled[:, part(t, wide)] * inverse
            numerator += dot(weights.astype(jnp.bfloat16), keys[part(t, wide), :])
            return numerator, fold(mass, weights, jnp.add)

        sums = (jnp.zeros((clusters, head_dim), jnp.float32), flat)
        numerator, mass = lax.fori_loop(0, tokens // wide, add, sums)
        mass_total = jnp.sum(mass, axis=1, keepdims=True)
        current[...] = numerator / mass_total
        potential[...] = pot + balance - (jnp.log2(peak) + jnp.log2(mass_total))

        @pl.when(jnp.min(peak) < SMALLEST_MASS)
        def _():
            def peaks(t, top):
                logits = logits_of(t, rounded, pot)
                row_peak = jnp.max(logits, axis=0, keepdims=True)
                total = jnp.sum(jnp.exp2(logits - row_peak), axis=0, keepdims=True)
                logprob = logits - (row_peak + jnp.log2(total))
                scaled[:, part(t, tile)] = logprob
                return jnp.maximum(top, jnp.max(logprob, axis=1, keepdims=True))

            lowest = jnp.full((clusters, 1), -jnp.inf, jnp.float32)
            top = lax.fori_loop(0, tokens // tile, peaks, lowest)

            def again(t, sums):
                numerator, mass = sums
                weights = jnp.exp2(scaled[:, part(t, wide)] - top)
                numerator += dot(weights.astype(jnp.bfloat16), keys[part(t, wide), :])
                return numerator, mass + jnp.sum(weights, axis=1, keepdims=True)

            zeros = (jnp.zeros((clusters, head_dim), jnp.float32), jnp.zeros_like(lowest))
            numerator, mass_total = lax.fori_loop(0, tokens // wide, again, zeros)
            current[...] = numerator / mass_total
            potential[...] = pot + balance - (top + jnp.log2(mass_total))

        return carry

    lax.fori_loop(0, ITERS, sweep, 0)
    shape = (cluster_dev, LANES)
    diagonal = lax.broadcasted_iota(jnp.int32, shape, 0) == lax.broadcasted_iota(
        jnp.int32, shape, 1
    )
    for s in range(sources):
        rows = slice(s * cluster_dev, (s + 1) * cluster_dev)
        outs[s][:cluster_dev, :] = current[rows, :]
        column = jnp.broadcast_to(potential[rows, :] * (1.0 / LOG2E), shape)
        line = jnp.sum(jnp.where(diagonal, column, 0.0), axis=0, keepdims=True)
        outs[s][cluster_dev:, :] = jnp.broadcast_to(line, (8, LANES))


def run_sweeps(blocks, tok_dev, cluster_dev):
    sources, head_dim = len(blocks), blocks[0].shape[1]
    tokens, clusters = sources * tok_dev, sources * cluster_dev
    return pl.pallas_call(
        functools.partial(sweeps_kernel, tok_dev, cluster_dev),
        out_shape=[jax.ShapeDtypeStruct((cluster_dev + 8, head_dim), jnp.float32)] * sources,
        in_specs=[VMEM] * sources,
        out_specs=[VMEM] * sources,
        scratch_shapes=[
            pltpu.VMEM((tokens, head_dim), jnp.bfloat16),
            pltpu.VMEM((clusters, head_dim), jnp.float32),
            pltpu.VMEM((clusters, 1), jnp.float32),
            pltpu.VMEM((clusters, tokens), jnp.float32),
        ],
        compiler_params=pltpu.CompilerParams(vmem_limit_bytes=40 * 2**20),
        cost_estimate=pl.CostEstimate(
            flops=64 * ITERS * tokens * clusters * head_dim,
            bytes_accessed=tokens * head_dim * 2,
            transcendentals=ITERS * tokens * clusters,
        ),
        name="sweeps",
    )(*blocks)


def gather_rows(index, first, idx_col_ref, rows_in, out_ref):
    count, tok_dev, _ = rows_in.shape
    chunks = out_ref.shape[1] // LANES
    tokens = lax.broadcasted_iota(jnp.int32, (LANES, tok_dev), 1)

    def gather(s, carry):
        k = index ^ (s + first)
        table = pltpu.roll(idx_col_ref[...], LANES - k * chunks, 1)
        values = rows_in[s]
        for r in range(chunks):
            picks = jnp.where(tokens == table[:, r : r + 1], 1.0, 0.0).astype(jnp.bfloat16)
            out_ref[s, r * LANES : (r + 1) * LANES, :] = dot(picks, values).astype(jnp.bfloat16)
        return carry

    lax.fori_loop(0, count, gather, 0)


def position_features(index, rows_in, at):
    sources, tok_dev, _ = rows_in.shape
    shape = (tok_dev, LANES)
    token = lax.broadcasted_iota(jnp.int32, shape, 0)
    lane = lax.broadcasted_iota(jnp.int32, shape, 1)
    fine = token & (DIGIT - 1)
    for s in range(sources):
        coarse = (token + (index ^ s) * tok_dev) >> 6
        for number, columns in enumerate(
            ((1, 1, 1, coarse, fine), (coarse * DIGIT, fine, 1, -DIGIT, -1))
        ):
            feature = jnp.zeros(shape, jnp.int32)
            for place, column in enumerate(columns):
                feature = jnp.where(lane == place, column, feature)
            start = at + number * LANES
            rows_in[s, :, start : start + LANES] = feature.astype(jnp.float32).astype(jnp.bfloat16)


def gather_keys_kernel(index_ref, *refs):
    blocks, (idx_col_ref, out_ref, rows_in) = refs[:-3], refs[-3:]
    head_dim = blocks[0].shape[1]
    for s, ref in enumerate(blocks):
        rows_in[s, :, :head_dim] = ref[: rows_in.shape[1], :]
    position_features(index_ref[0], rows_in, head_dim)
    gather_rows(index_ref[0], 0, idx_col_ref, rows_in, out_ref)


def gather_near_kernel(index_ref, *refs):
    blocks, (idx_col_ref, out_ref, rows_in) = refs[:-3], refs[-3:]
    for s, ref in enumerate(blocks):
        rows_in[s] = ref[...]
    gather_rows(index_ref[0], 0, idx_col_ref, rows_in, out_ref)


def attention_kernel(segment, group, index_ref, after_ref, *refs):
    far = (len(refs) - 7) // 3
    sources = 2 * far
    blocks = refs[:far]
    near_ref, gk_ref, idx_col_ref, idx_row_ref = refs[far : far + 4]
    outs = refs[far + 4 : far + 4 + sources]
    rows_in, gathered, blended = refs[far + 4 + sources :]
    tok_dev, head_dim = rows_in.shape[1], outs[0].shape[1]
    slots = gk_ref.shape[1]
    block = sources * TILE
    scale = head_dim**-0.5 * LOG2E
    for s, ref in enumerate(blocks):
        rows_in[s] = ref[...]
    gather_rows(index_ref[0], far, idx_col_ref, rows_in, gathered)

    row_cluster = lax.broadcasted_iota(jnp.int32, (block, block), 0) % TILE // segment
    col_cluster = lax.broadcasted_iota(jnp.int32, (block, block), 1) % TILE // segment
    same = row_cluster == col_cluster
    flat = (block, head_dim)

    def attend(step, carry):
        rows = [
            pl.ds(pl.multiple_of((step * group + u) * TILE, TILE), TILE) for u in range(group)
        ]
        both = [jnp.concatenate([near_ref[:, r, :], gathered[:, r, :]], axis=0) for r in rows]
        keys = [gk_ref[:, r, :] for r in rows]

        def piece(values, number):
            at = number * head_dim
            return values[:, :, at : at + head_dim].reshape(flat)

        def against(left, right):
            return lax.dot_general(left, right, BY_ROWS, preferred_element_type=jnp.float32)

        ahead = [against(piece(k, 2), piece(k, 1)) for k in keys]
        scores = [
            jnp.where(
                same & (ahead[u] >= 1.0),
                against(piece(both[u], 0), piece(keys[u], 0)) * scale,
                -1e30,
            )
            for u in range(group)
        ]
        tops = [jnp.max(s, axis=1, keepdims=True) for s in scores]
        unnormed = [jnp.exp2(s - t) for s, t in zip(scores, tops)]
        totals = [jnp.sum(u, axis=1, keepdims=True) for u in unnormed]
        mixed = [
            dot(unnormed[u].astype(jnp.bfloat16), piece(both[u], 1))
            * (1.0 / totals[u])
            for u in range(group)
        ]
        for u in range(group):
            blended[:, rows[u], :] = (
                mixed[u].astype(jnp.bfloat16).reshape(sources, TILE, head_dim)
            )
        return carry

    lax.fori_loop(0, slots // TILE // group, attend, 0)

    tokens = lax.broadcasted_iota(jnp.int32, (tok_dev, slots), 0)
    for s in range(sources):
        wanted = idx_row_ref[pl.ds(index_ref[0] ^ s, 1), :]
        picks = jnp.where(tokens == wanted, 1.0, 0.0).astype(jnp.bfloat16)
        rows = dot(picks, blended[s]).astype(jnp.bfloat16)
        outs[s][:tok_dev, :] = rows
        wide = rows.astype(jnp.float32)
        squares = jnp.sum((wide * wide).T, axis=0, keepdims=True)
        lines = [squares[:, p : p + LANES] for p in range(0, tok_dev, LANES)]
        coarse = [line.astype(jnp.bfloat16).astype(jnp.float32) for line in lines]
        fine = [line - high for line, high in zip(lines, coarse)]
        spare = [jnp.zeros_like(lines[0])] * (TILE - 2 * len(lines))
        outs[s][tok_dev:, :] = jnp.concatenate(coarse + fine + spare, axis=0).astype(jnp.bfloat16)


def tables_kernel(tok_dev, segment, *refs):
    blocks, (idx_col_ref, idx_row_ref) = refs[:-2], refs[-2:]
    sources = len(blocks)
    width = sources * segment
    square = (LANES, LANES)
    row = lax.broadcasted_iota(jnp.int32, square, 0)
    lane = lax.broadcasted_iota(jnp.int32, square, 1)

    def ones_where(condition):
        return jnp.where(condition, 1.0, 0.0)

    spread = ones_where(row[:, :width] // segment == lane[:, :width]).astype(jnp.bfloat16)
    mine = (lane % segment == row % segment) & (lane < 2 * width)
    weight = jnp.where(row < width, float(DIGIT), 1.0) * ones_where(row < 2 * width)
    slot_of = row % width // segment
    columns = jnp.zeros(square, jnp.float32)
    by_row = (weight * ones_where(slot_of == lane))[:, :sources].T.astype(jnp.bfloat16)
    for r, block in enumerate(blocks):
        spread_digits = dot(spread, block[-width:, :])
        digits = jnp.where(mine, spread_digits, 0.0).astype(jnp.bfloat16)
        place = (lane // sources == slot_of) & (lane % sources == r)
        columns += dot(digits, (weight * ones_where(place)).astype(jnp.bfloat16))
        line = lax.dot_general(by_row, digits, BY_ROWS, preferred_element_type=jnp.float32)
        idx_row_ref[:, r * LANES : (r + 1) * LANES] = line.astype(jnp.int32) - tok_dev * row[:sources]
    idx_col_ref[...] = columns.astype(jnp.int32) - tok_dev * (lane // sources)


def run_tables(blocks, tok_dev, segment):
    sources = len(blocks)
    return pl.pallas_call(
        functools.partial(tables_kernel, tok_dev, segment),
        out_shape=(
            jax.ShapeDtypeStruct((LANES, LANES), jnp.int32),
            jax.ShapeDtypeStruct((sources, sources * LANES), jnp.int32),
        ),
        in_specs=[VMEM] * sources,
        out_specs=(VMEM, VMEM),
        compiler_params=pltpu.CompilerParams(vmem_limit_bytes=8 * 2**20),
        name="tables",
    )(*blocks)


def run_attention(index, after, key_blocks, pair_blocks, tables, tok_dev, segment, group=8):
    sources, head_dim = len(key_blocks), key_blocks[0].shape[1]
    idx_col, idx_row = tables
    slots = idx_row.shape[1]
    flops = 2 * sources * slots * tok_dev * head_dim
    gathered_keys = pl.pallas_call(
        gather_keys_kernel,
        out_shape=jax.ShapeDtypeStruct((sources, slots, 3 * head_dim), jnp.bfloat16),
        in_specs=[SMEM] + [VMEM] * (sources + 1),
        out_specs=VMEM,
        scratch_shapes=[pltpu.VMEM((sources, tok_dev, 3 * head_dim), jnp.bfloat16)],
        compiler_params=pltpu.CompilerParams(vmem_limit_bytes=24 * 2**20),
        cost_estimate=pl.CostEstimate(
            flops=4 * flops, bytes_accessed=6 * sources * tok_dev * head_dim, transcendentals=0
        ),
        name="gather_keys",
    )(index, *key_blocks, idx_col)
    near = sources // 2
    gathered_near = pl.pallas_call(
        gather_near_kernel,
        out_shape=jax.ShapeDtypeStruct((near, slots, 2 * head_dim), jnp.bfloat16),
        in_specs=[SMEM] + [VMEM] * (near + 1),
        out_specs=VMEM,
        scratch_shapes=[pltpu.VMEM((near, tok_dev, 2 * head_dim), jnp.bfloat16)],
        compiler_params=pltpu.CompilerParams(vmem_limit_bytes=24 * 2**20),
        cost_estimate=pl.CostEstimate(
            flops=4 * flops, bytes_accessed=6 * sources * tok_dev * head_dim, transcendentals=0
        ),
        name="gather_near",
    )(index, *pair_blocks[:near], idx_col)
    return pl.pallas_call(
        functools.partial(attention_kernel, segment, group),
        out_shape=[jax.ShapeDtypeStruct((tok_dev + TILE, head_dim), jnp.bfloat16)] * sources,
        in_specs=[SMEM, pl.BlockSpec(memory_space=pl.ANY)] + [VMEM] * (near + 4),
        out_specs=[VMEM] * sources,
        scratch_shapes=[
            pltpu.VMEM((near, tok_dev, 2 * head_dim), jnp.bfloat16),
            pltpu.VMEM((near, slots, 2 * head_dim), jnp.bfloat16),
            pltpu.VMEM((sources, slots, head_dim), jnp.bfloat16),
        ],
        compiler_params=pltpu.CompilerParams(vmem_limit_bytes=40 * 2**20),
        cost_estimate=pl.CostEstimate(
            flops=8 * flops,
            bytes_accessed=8 * sources * tok_dev * head_dim,
            transcendentals=slots // TILE * (sources * TILE) ** 2,
        ),
        name="attention",
    )(index, after, *pair_blocks[near:], gathered_near, gathered_keys, idx_col, idx_row)


def sum_squares_kernel(lines, *refs):
    total = sum(ref[-TILE:, :].astype(jnp.float32) for ref in refs[:-1])
    refs[-1][...] = total[:lines, :] + total[lines : 2 * lines, :]


def sum_squares(parts, tok_dev):
    lines = tok_dev // LANES
    return pl.pallas_call(
        functools.partial(sum_squares_kernel, lines),
        out_shape=jax.ShapeDtypeStruct((lines, LANES), jnp.float32),
        in_specs=[VMEM] * len(parts),
        out_specs=VMEM,
        compiler_params=pltpu.CompilerParams(vmem_limit_bytes=8 * 2**20),
        name="sum_squares",
    )(*parts)


def collect_kernel(index_ref, *refs):
    parts, (out_ref, pot_ref) = refs[:-2], refs[-2:]
    cluster_dev = out_ref.shape[1]
    for s, ref in enumerate(parts):
        head = index_ref[0] ^ s
        out_ref[head] = ref[:cluster_dev, :]
        pot_ref[pl.ds(head, 1), :] = ref[cluster_dev : cluster_dev + 1, :]


def collect(index, parts, cluster_dev):
    return pl.pallas_call(
        collect_kernel,
        out_shape=(
            jax.ShapeDtypeStruct((len(parts), cluster_dev, LANES), jnp.float32),
            jax.ShapeDtypeStruct((len(parts), LANES), jnp.float32),
        ),
        in_specs=[SMEM] + [VMEM] * len(parts),
        out_specs=(VMEM, VMEM),
        compiler_params=pltpu.CompilerParams(vmem_limit_bytes=8 * 2**20),
        name="collect",
    )(index, *parts)


def norm_kernel(width, heads, index_ref, *refs):
    parts, squares, (gain_ref, out_ref) = refs[:heads], refs[heads:-2], refs[-2:]
    head_dim = parts[0].shape[1]
    total = sum(ref[...] for ref in squares)
    inverse = lax.rsqrt(total / width + 1e-06)
    columns = [
        jnp.broadcast_to(inverse[p : p + 1, :], (LANES, LANES)).T for p in range(total.shape[0])
    ]
    for s, ref in enumerate(parts):
        head = index_ref[0] ^ s
        lanes = pl.ds(pl.multiple_of(head * head_dim, head_dim), head_dim)
        gain = gain_ref[:, lanes]
        for p, column in enumerate(columns):
            rows = slice(p * LANES, (p + 1) * LANES)
            out_ref[rows, lanes] = (ref[rows, :].astype(jnp.float32) * column * gain).astype(
                jnp.bfloat16
            )


def run_norm(index, parts, squares, gain, width, tok_dev):
    head_dim = parts[0].shape[1]
    return pl.pallas_call(
        functools.partial(norm_kernel, width, len(parts)),
        out_shape=jax.ShapeDtypeStruct((tok_dev, len(parts) * head_dim), jnp.bfloat16),
        in_specs=[SMEM] + [VMEM] * (len(parts) + len(squares) + 1),
        out_specs=VMEM,
        compiler_params=pltpu.CompilerParams(vmem_limit_bytes=24 * 2**20),
        name="norm",
    )(index, *parts, *squares, gain.reshape(1, -1))


def pack_kernel(index_ref, key_ref, centroid_ref, list_ref, count_ref, *outs):
    tok_dev = key_ref.shape[0]
    _, cluster_dev, head_dim = centroid_ref.shape
    width, sources = list_ref.shape[2], count_ref.shape[1]
    segment = width // sources
    owner = lax.broadcasted_iota(jnp.int32, (sources, width), 1) // segment
    spread = jnp.where(
        owner == lax.broadcasted_iota(jnp.int32, (sources, width), 0), 1.0, 0.0
    ).astype(jnp.bfloat16)
    slot = lax.broadcasted_iota(jnp.int32, (cluster_dev, width), 1) % segment
    at = lax.broadcasted_iota(jnp.int32, (width, head_dim), 1)
    source = lax.broadcasted_iota(jnp.int32, (width, head_dim), 0)
    first = jnp.where(at == source, 1.0, 0.0).astype(jnp.bfloat16)
    second = jnp.where(at == source + width, 1.0, 0.0).astype(jnp.bfloat16)
    for s, out in enumerate(outs):
        head = index_ref[0] ^ s
        lanes = pl.ds(pl.multiple_of(head * head_dim, head_dim), head_dim)
        out[:tok_dev, :] = key_ref[:, lanes]
        out[tok_dev : tok_dev + cluster_dev, :] = centroid_ref[head].astype(jnp.bfloat16)
        counts = lax.dot_general(
            count_ref[head].astype(jnp.float32).astype(jnp.bfloat16), spread,
            (((0,), (0,)), ((), ())), preferred_element_type=jnp.float32,
        )
        marked = jnp.where(slot.astype(jnp.float32) < counts, list_ref[head], -TILE)
        coarse = (marked >> 6).astype(jnp.float32).astype(jnp.bfloat16)
        fine = (marked & (DIGIT - 1)).astype(jnp.float32).astype(jnp.bfloat16)
        out[tok_dev + cluster_dev :, :] = (dot(coarse, first) + dot(fine, second)).astype(
            jnp.bfloat16
        )


def pack_keys(index, key_rows, centroids, cluster_lists, live_counts):
    heads, cluster_dev, head_dim = centroids.shape
    rows = key_rows.shape[0] + 2 * cluster_dev
    return pl.pallas_call(
        pack_kernel,
        out_shape=[jax.ShapeDtypeStruct((rows, head_dim), jnp.bfloat16)] * heads,
        in_specs=[SMEM] + [VMEM] * 4,
        out_specs=[VMEM] * heads,
        compiler_params=pltpu.CompilerParams(vmem_limit_bytes=60 * 2**20),
        name="pack_keys",
    )(index, key_rows, centroids, cluster_lists, live_counts.transpose(0, 2, 1))


def shift_ring(size, step):
    return [(j, (j + step) % size) for j in range(size)]


def far_first(size):
    return list(range(size // 2, size)) + list(range(1, size // 2))


def pack_kernel(index_ref, key_ref, centroid_ref, list_ref, count_ref, *outs):
    tok_dev = key_ref.shape[0]
    _, cluster_dev, head_dim = centroid_ref.shape
    width, sources = list_ref.shape[2], count_ref.shape[1]
    segment = width // sources
    owner = lax.broadcasted_iota(jnp.int32, (sources, width), 1) // segment
    spread = jnp.where(
        owner == lax.broadcasted_iota(jnp.int32, (sources, width), 0), 1.0, 0.0
    ).astype(jnp.bfloat16)
    slot = lax.broadcasted_iota(jnp.int32, (cluster_dev, width), 1) % segment
    at = lax.broadcasted_iota(jnp.int32, (width, head_dim), 1)
    source = lax.broadcasted_iota(jnp.int32, (width, head_dim), 0)
    first = jnp.where(at == source, 1.0, 0.0).astype(jnp.bfloat16)
    second = jnp.where(at == source + width, 1.0, 0.0).astype(jnp.bfloat16)
    for s, out in enumerate(outs):
        head = index_ref[0] ^ s
        lanes = pl.ds(pl.multiple_of(head * head_dim, head_dim), head_dim)
        out[:tok_dev, :] = key_ref[:, lanes]
        out[tok_dev : tok_dev + cluster_dev, :] = centroid_ref[head].astype(jnp.bfloat16)
        counts = lax.dot_general(
            count_ref[head].astype(jnp.float32).astype(jnp.bfloat16), spread,
            (((0,), (0,)), ((), ())), preferred_element_type=jnp.float32,
        )
        marked = jnp.where(slot.astype(jnp.float32) < counts, list_ref[head], -TILE)
        coarse = (marked >> 6).astype(jnp.float32).astype(jnp.bfloat16)
        fine = (marked & (DIGIT - 1)).astype(jnp.float32).astype(jnp.bfloat16)
        out[tok_dev + cluster_dev :, :] = (dot(coarse, first) + dot(fine, second)).astype(
            jnp.bfloat16
        )


def pack_keys(index, key_rows, centroids, cluster_lists, live_counts):
    heads, cluster_dev, head_dim = centroids.shape
    rows = key_rows.shape[0] + 2 * cluster_dev
    return pl.pallas_call(
        pack_kernel,
        out_shape=[jax.ShapeDtypeStruct((rows, head_dim), jnp.bfloat16)] * heads,
        in_specs=[SMEM] + [VMEM] * 4,
        out_specs=[VMEM] * heads,
        compiler_params=pltpu.CompilerParams(vmem_limit_bytes=60 * 2**20),
        name="pack_keys",
    )(index, key_rows, centroids, cluster_lists, live_counts.transpose(0, 2, 1))


def shift_ring(size, step):
    return [(j, (j + step) % size) for j in range(size)]


def exchange(blocks):
    size = len(blocks)
    arrived = list(blocks)
    for s in far_first(size):
        arrived[s] = lax.ppermute(blocks[s], "ctx", [(j, j ^ s) for j in range(size)])
    return arrived


def local(query_rows, key_rows, value_rows, centroids, norm_gain, cluster_lists, live_counts):
    context_length = lax.axis_size("ctx")
    head_dev = centroids.shape[0]
    if head_dev != context_length or context_length & (context_length - 1):
        return local_wide(
            query_rows, key_rows, value_rows, centroids, norm_gain, cluster_lists, live_counts
        )
    return local_heads(
        query_rows, key_rows, value_rows, centroids, norm_gain, cluster_lists, live_counts
    )


def local_heads(query_rows, key_rows, value_rows, centroids, norm_gain, cluster_lists, live_counts):
    context_length = lax.axis_size("ctx")
    head_size = lax.axis_size("head")
    tok_dev = query_rows.shape[0]
    head_dev, cluster_dev, head_dim = centroids.shape
    segment = cluster_lists.shape[2] // context_length
    index = lax.axis_index("ctx")
    place = index.astype(jnp.int32).reshape(1)

    def by_head(rows):
        return rows.reshape(tok_dev, head_dev, head_dim).transpose(1, 0, 2)

    pairs = jnp.concatenate([by_head(query_rows), by_head(value_rows)], axis=2)
    pairs = [
        lax.dynamic_index_in_dim(pairs, index ^ s, 0, keepdims=False)
        for s in range(context_length)
    ]
    key_blocks = exchange(pack_keys(place, key_rows, centroids, cluster_lists, live_counts))
    pair_blocks = exchange(pairs)
    tables = run_tables(key_blocks, tok_dev, segment)
    swept = run_sweeps(key_blocks, tok_dev, cluster_dev)
    outs = run_attention(place, swept[0], key_blocks, pair_blocks, tables, tok_dev, segment)
    parts = exchange(outs)
    swept_mine, potential_mine = collect(place, exchange(swept), cluster_dev)
    mine = sum_squares(parts, tok_dev)
    squares = [mine] + [
        lax.ppermute(mine, "head", shift_ring(head_size, step)) for step in range(1, head_size)
    ]
    features = head_dev * head_dim * head_size
    normalized = run_norm(place, parts, squares, norm_gain, features, tok_dev)
    return (normalized, swept_mine, potential_mine[:, :cluster_dev])


def solution(mesh):
    placed = (
        P("ctx", "head"),
        P("ctx", "head"),
        P("ctx", "head"),
        P("head", "ctx", None),
        P("head"),
        P("head", "ctx", None),
        P("head", "ctx", None),
    )
    return jax.shard_map(
        local,
        mesh=mesh,
        in_specs=placed,
        out_specs=(P("ctx", "head"), P("head", "ctx", None), P("head", "ctx")),
        check_vma=False,
    )
```

```python
import functools
import math

import jax
import jax.numpy as jnp
from jax import lax
from jax.experimental import pallas as pl
from jax.experimental.pallas import tpu as pltpu
from jax.sharding import PartitionSpec as P

ITERS = 5
LOG2E = math.log2(math.e)
TILE = 16
DIGIT = 64
LANES = 128
SMALLEST_MASS = 2.0**-80
VMEM = pl.BlockSpec(memory_space=pltpu.VMEM)
SMEM = pl.BlockSpec(memory_space=pltpu.SMEM)
BY_ROWS = (((1,), (1,)), ((), ()))


def block_attention(block_item):
    block_rows, positions, is_live = block_item
    head_dim = block_rows.shape[1] // 3
    query_part = block_rows[:, :head_dim]
    key_part = block_rows[:, head_dim : 2 * head_dim]
    value_part = block_rows[:, 2 * head_dim :]
    scores = lax.dot_general(
        query_part, key_part, (((1,), (1,)), ((), ())), preferred_element_type=jnp.float32
    ) * head_dim ** (-0.5)
    allowed = is_live[None, :] & (positions[None, :] <= positions[:, None])
    scores = jnp.where(allowed, scores, -1e30)
    peak_row = jnp.max(scores, axis=-1, keepdims=True)
    unnormed = jnp.exp(scores - peak_row)
    row_total = jnp.sum(unnormed, axis=-1, keepdims=True)
    blended = jnp.dot(unnormed.astype(jnp.bfloat16), value_part, preferred_element_type=jnp.float32)
    return (blended / row_total).astype(jnp.bfloat16)


def attend_blocks(block_rows, cluster_lists, owned_live):
    count_blocks = block_rows.shape[0]
    positions = cluster_lists.reshape(count_blocks, -1)
    is_live = owned_live.reshape(count_blocks, -1)
    return lax.map(block_attention, (block_rows, positions, is_live))


def balancing_sweeps(per_head_keys, centroids, device_index, context_length):
    head_dev, cluster_dev, head_dim = centroids.shape
    clusters = cluster_dev * context_length
    tok_dev = per_head_keys.shape[0]
    balance = math.log(tok_dev * context_length / clusters)
    rounded = lax.all_gather(centroids.astype(jnp.bfloat16), "ctx", axis=1, tiled=True)
    potential = jnp.zeros((head_dev, clusters), jnp.float32)
    current_mine = centroids
    for _ in range(ITERS):
        logits = (
            jnp.einsum("thd,hcd->thc", per_head_keys, rounded, preferred_element_type=jnp.float32)
            * head_dim ** (-0.5)
            + potential[None]
        )
        row_peak = jnp.max(logits, axis=-1, keepdims=True)
        log_total = row_peak + jnp.log(jnp.sum(jnp.exp(logits - row_peak), axis=-1, keepdims=True))
        logprob = logits - log_total
        column_peak = lax.pmax(jnp.max(logprob, axis=0), "ctx")
        weights = jnp.exp(logprob - column_peak[None])
        local_mass = jnp.sum(weights, axis=0)
        local_numerator = jnp.einsum(
            "thc,thd->hcd",
            weights.astype(jnp.bfloat16),
            per_head_keys,
            preferred_element_type=jnp.float32,
        )
        mass_total, numerator = lax.psum((local_mass, local_numerator), "ctx")
        current = numerator / mass_total[:, :, None]
        rounded = current.astype(jnp.bfloat16)
        current_mine = lax.dynamic_slice_in_dim(current, device_index * cluster_dev, cluster_dev, 1)
        potential = potential + balance - (column_peak + jnp.log(mass_total))
    return (
        current_mine,
        lax.dynamic_slice_in_dim(potential, device_index * cluster_dev, cluster_dev, 1),
    )


def local_wide(query_rows, key_rows, value_rows, centroids, norm_gain, cluster_lists, live_counts):
    context_length = lax.axis_size("ctx")
    device_index = lax.axis_index("ctx")
    tok_dev = query_rows.shape[0]
    head_dev, cluster_dev, head_dim = centroids.shape
    segment = cluster_lists.shape[2] // context_length
    query_heads = query_rows.reshape(tok_dev, head_dev, head_dim)
    per_head_keys = key_rows.reshape(tok_dev, head_dev, head_dim)
    value_heads = value_rows.reshape(tok_dev, head_dev, head_dim)
    swept_centroids, potentials = balancing_sweeps(
        per_head_keys, centroids, device_index, context_length
    )
    lists_split = cluster_lists.reshape(head_dev, cluster_dev, context_length, segment)
    asked_ids, asked_counts = (
        lax.all_to_all(lists_split, "ctx", split_axis=2, concat_axis=2, tiled=True),
        lax.all_to_all(live_counts, "ctx", split_axis=2, concat_axis=2, tiled=True),
    )
    slot_ids = jnp.arange(segment, dtype=jnp.int32)
    asked_live = slot_ids < asked_counts[..., None]
    local_ids = jnp.where(asked_live, asked_ids - device_index * tok_dev, 0)
    head_ids = jnp.broadcast_to(
        jnp.arange(head_dev, dtype=jnp.int32)[:, None, None, None], local_ids.shape
    )
    owned_live = slot_ids < live_counts[..., None]
    empty_out = jnp.zeros((tok_dev, head_dev, head_dim), jnp.bfloat16)
    sent_rows = jnp.concatenate(
        [
            query_heads[local_ids, head_ids],
            per_head_keys[local_ids, head_ids],
            value_heads[local_ids, head_ids],
        ],
        axis=-1,
    )
    arrived = lax.all_to_all(sent_rows, "ctx", split_axis=2, concat_axis=2, tiled=True)
    block_rows = arrived.reshape(head_dev * cluster_dev, context_length * segment, 3 * head_dim)
    block_out = attend_blocks(block_rows, cluster_lists, owned_live)
    returned = lax.all_to_all(
        block_out.reshape(head_dev, cluster_dev, context_length, segment, head_dim),
        "ctx",
        split_axis=2,
        concat_axis=2,
        tiled=True,
    )
    target = jnp.where(asked_live, local_ids, tok_dev)
    attended = empty_out.at[target, head_ids].set(returned, mode="drop")
    wide_attended = attended.reshape(tok_dev, head_dev * head_dim).astype(jnp.float32)
    squares = lax.psum(jnp.sum(wide_attended * wide_attended, axis=-1), "head")
    width = head_dev * head_dim * lax.axis_size("head")
    normalized = (wide_attended * lax.rsqrt(squares / width + 1e-06)[:, None] * norm_gain).astype(
        jnp.bfloat16
    )
    return (normalized, swept_centroids, potentials)


def dot(a, b):
    return jnp.dot(a, b, preferred_element_type=jnp.float32)


def sweeps_kernel(tok_dev, cluster_dev, *refs):
    sources = (len(refs) - 4) // 2
    blocks, outs = refs[:sources], refs[sources : 2 * sources]
    keys, current, potential, scaled = refs[-4:]
    tokens, head_dim = keys.shape
    clusters = sources * cluster_dev
    scale = head_dim**-0.5 * LOG2E
    balance = math.log2(tokens / clusters)
    tile, wide = 2 * tok_dev, min(4, sources) * tok_dev
    for s, block in enumerate(blocks):
        keys[s * tok_dev : (s + 1) * tok_dev, :] = block[:tok_dev, :]
        current[s * cluster_dev : (s + 1) * cluster_dev, :] = block[
            tok_dev : tok_dev + cluster_dev, :
        ].astype(jnp.float32)
    potential[...] = jnp.zeros_like(potential)

    def part(t, size):
        return pl.ds(pl.multiple_of(t * size, size), size)

    def logits_of(t, rounded, pot):
        return (
            lax.dot_general(
                rounded, keys[part(t, tile), :], BY_ROWS, preferred_element_type=jnp.float32
            )
            * scale
            + pot
        )

    def fold(total, values, op):
        for p in range(values.shape[1] // LANES):
            total = op(total, values[:, p * LANES : (p + 1) * LANES])
        return total

    def sweep(_, carry):
        rounded = current[...].astype(jnp.bfloat16)
        pot = potential[...]
        flat = jnp.zeros((clusters, LANES), jnp.float32)

        def members(t, peak):
            logits = logits_of(t, rounded, pot)
            shifted = jnp.exp2(logits - jnp.max(logits, axis=0, keepdims=True))
            member = shifted * (1.0 / jnp.sum(shifted, axis=0, keepdims=True))
            scaled[:, part(t, tile)] = member
            return fold(peak, member, jnp.maximum)

        peak = jnp.max(
            lax.fori_loop(0, tokens // tile, members, flat), axis=1, keepdims=True
        )
        inverse = 1.0 / jnp.maximum(peak, SMALLEST_MASS)

        def add(t, sums):
            numerator, mass = sums
            weights = scaled[:, part(t, wide)] * inverse
            numerator += dot(weights.astype(jnp.bfloat16), keys[part(t, wide), :])
            return numerator, fold(mass, weights, jnp.add)

        sums = (jnp.zeros((clusters, head_dim), jnp.float32), flat)
        numerator, mass = lax.fori_loop(0, tokens // wide, add, sums)
        mass_total = jnp.sum(mass, axis=1, keepdims=True)
        current[...] = numerator / mass_total
        potential[...] = pot + balance - (jnp.log2(peak) + jnp.log2(mass_total))

        @pl.when(jnp.min(peak) < SMALLEST_MASS)
        def _():
            def peaks(t, top):
                logits = logits_of(t, rounded, pot)
                row_peak = jnp.max(logits, axis=0, keepdims=True)
                total = jnp.sum(jnp.exp2(logits - row_peak), axis=0, keepdims=True)
                logprob = logits - (row_peak + jnp.log2(total))
                scaled[:, part(t, tile)] = logprob
                return jnp.maximum(top, jnp.max(logprob, axis=1, keepdims=True))

            lowest = jnp.full((clusters, 1), -jnp.inf, jnp.float32)
            top = lax.fori_loop(0, tokens // tile, peaks, lowest)

            def again(t, sums):
                numerator, mass = sums
                weights = jnp.exp2(scaled[:, part(t, wide)] - top)
                numerator += dot(weights.astype(jnp.bfloat16), keys[part(t, wide), :])
                return numerator, mass + jnp.sum(weights, axis=1, keepdims=True)

            zeros = (jnp.zeros((clusters, head_dim), jnp.float32), jnp.zeros_like(lowest))
            numerator, mass_total = lax.fori_loop(0, tokens // wide, again, zeros)
            current[...] = numerator / mass_total
            potential[...] = pot + balance - (top + jnp.log2(mass_total))

        return carry

    lax.fori_loop(0, ITERS, sweep, 0)
    shape = (cluster_dev, LANES)
    diagonal = lax.broadcasted_iota(jnp.int32, shape, 0) == lax.broadcasted_iota(
        jnp.int32, shape, 1
    )
    for s in range(sources):
        rows = slice(s * cluster_dev, (s + 1) * cluster_dev)
        outs[s][:cluster_dev, :] = current[rows, :]
        column = jnp.broadcast_to(potential[rows, :] * (1.0 / LOG2E), shape)
        line = jnp.sum(jnp.where(diagonal, column, 0.0), axis=0, keepdims=True)
        outs[s][cluster_dev:, :] = jnp.broadcast_to(line, (8, LANES))


def run_sweeps(blocks, tok_dev, cluster_dev):
    sources, head_dim = len(blocks), blocks[0].shape[1]
    tokens, clusters = sources * tok_dev, sources * cluster_dev
    return pl.pallas_call(
        functools.partial(sweeps_kernel, tok_dev, cluster_dev),
        out_shape=[jax.ShapeDtypeStruct((cluster_dev + 8, head_dim), jnp.float32)] * sources,
        in_specs=[VMEM] * sources,
        out_specs=[VMEM] * sources,
        scratch_shapes=[
            pltpu.VMEM((tokens, head_dim), jnp.bfloat16),
            pltpu.VMEM((clusters, head_dim), jnp.float32),
            pltpu.VMEM((clusters, 1), jnp.float32),
            pltpu.VMEM((clusters, tokens), jnp.float32),
        ],
        compiler_params=pltpu.CompilerParams(vmem_limit_bytes=40 * 2**20),
        cost_estimate=pl.CostEstimate(
            flops=64 * ITERS * tokens * clusters * head_dim,
            bytes_accessed=tokens * head_dim * 2,
            transcendentals=ITERS * tokens * clusters,
        ),
        name="sweeps",
    )(*blocks)


def gather_rows(index, first, idx_col_ref, rows_in, out_ref):
    count, tok_dev, _ = rows_in.shape
    chunks = out_ref.shape[1] // LANES
    tokens = lax.broadcasted_iota(jnp.int32, (LANES, tok_dev), 1)

    def gather(s, carry):
        k = index ^ (s + first)
        table = pltpu.roll(idx_col_ref[...], LANES - k * chunks, 1)
        values = rows_in[s]
        for r in range(chunks):
            picks = jnp.where(tokens == table[:, r : r + 1], 1.0, 0.0).astype(jnp.bfloat16)
            out_ref[s, r * LANES : (r + 1) * LANES, :] = dot(picks, values).astype(jnp.bfloat16)
        return carry

    lax.fori_loop(0, count, gather, 0)


def position_features(index, rows_in, at):
    sources, tok_dev, _ = rows_in.shape
    shape = (tok_dev, LANES)
    token = lax.broadcasted_iota(jnp.int32, shape, 0)
    lane = lax.broadcasted_iota(jnp.int32, shape, 1)
    fine = token & (DIGIT - 1)
    for s in range(sources):
        coarse = (token + (index ^ s) * tok_dev) >> 6
        for number, columns in enumerate(
            ((1, 1, 1, coarse, fine), (coarse * DIGIT, fine, 1, -DIGIT, -1))
        ):
            feature = jnp.zeros(shape, jnp.int32)
            for place, column in enumerate(columns):
                feature = jnp.where(lane == place, column, feature)
            start = at + number * LANES
            rows_in[s, :, start : start + LANES] = feature.astype(jnp.float32).astype(jnp.bfloat16)


def gather_keys_kernel(index_ref, *refs):
    blocks, (idx_col_ref, out_ref, rows_in) = refs[:-3], refs[-3:]
    head_dim = blocks[0].shape[1]
    for s, ref in enumerate(blocks):
        rows_in[s, :, :head_dim] = ref[: rows_in.shape[1], :]
    position_features(index_ref[0], rows_in, head_dim)
    gather_rows(index_ref[0], 0, idx_col_ref, rows_in, out_ref)


def gather_pairs_kernel(first, index_ref, *refs):
    blocks, (idx_col_ref, out_ref, rows_in) = refs[:-3], refs[-3:]
    for s, ref in enumerate(blocks):
        rows_in[s] = ref[...]
    gather_rows(index_ref[0], first, idx_col_ref, rows_in, out_ref)


def gather_pairs(index, blocks, idx_col, first, slots):
    count, (tok_dev, width) = len(blocks), blocks[0].shape
    return pl.pallas_call(
        functools.partial(gather_pairs_kernel, first),
        out_shape=jax.ShapeDtypeStruct((count, slots, width), jnp.bfloat16),
        in_specs=[SMEM] + [VMEM] * (count + 1),
        out_specs=VMEM,
        scratch_shapes=[pltpu.VMEM((count, tok_dev, width), jnp.bfloat16)],
        compiler_params=pltpu.CompilerParams(vmem_limit_bytes=24 * 2**20),
        cost_estimate=pl.CostEstimate(
            flops=4 * count * slots * tok_dev * width,
            bytes_accessed=6 * count * tok_dev * width,
            transcendentals=0,
        ),
        name="gather_pairs",
    )(index, *blocks, idx_col)


def attention_kernel(segment, group, early_count, index_ref, after_ref, last_ref, *refs):
    early = refs[:early_count]
    gk_ref, idx_col_ref, idx_row_ref = refs[early_count : early_count + 3]
    outs = refs[early_count + 3 : -3]
    rows_in, gathered, blended = refs[-3:]
    sources = len(outs)
    tok_dev, head_dim = rows_in.shape[1], outs[0].shape[1]
    slots = gk_ref.shape[1]
    block = sources * TILE
    scale = head_dim**-0.5 * LOG2E
    rows_in[0] = last_ref[...]
    gather_rows(index_ref[0], sources - 1, idx_col_ref, rows_in, gathered)

    row_cluster = lax.broadcasted_iota(jnp.int32, (block, block), 0) % TILE // segment
    col_cluster = lax.broadcasted_iota(jnp.int32, (block, block), 1) % TILE // segment
    same = row_cluster == col_cluster
    flat = (block, head_dim)

    def attend(step, carry):
        rows = [
            pl.ds(pl.multiple_of((step * group + u) * TILE, TILE), TILE) for u in range(group)
        ]
        both = [
            jnp.concatenate([part[:, r, :] for part in (*early, gathered)], axis=0) for r in rows
        ]
        keys = [gk_ref[:, r, :] for r in rows]

        def piece(values, number):
            at = number * head_dim
            return values[:, :, at : at + head_dim].reshape(flat)

        def against(left, right):
            return lax.dot_general(left, right, BY_ROWS, preferred_element_type=jnp.float32)

        ahead = [against(piece(k, 2), piece(k, 1)) for k in keys]
        scores = [
            jnp.where(
                same & (ahead[u] >= 1.0),
                against(piece(both[u], 0), piece(keys[u], 0)) * scale,
                -1e30,
            )
            for u in range(group)
        ]
        tops = [jnp.max(s, axis=1, keepdims=True) for s in scores]
        unnormed = [jnp.exp2(s - t) for s, t in zip(scores, tops)]
        totals = [jnp.sum(u, axis=1, keepdims=True) for u in unnormed]
        mixed = [
            dot(unnormed[u].astype(jnp.bfloat16), piece(both[u], 1))
            * (1.0 / totals[u])
            for u in range(group)
        ]
        for u in range(group):
            blended[:, rows[u], :] = (
                mixed[u].astype(jnp.bfloat16).reshape(sources, TILE, head_dim)
            )
        return carry

    lax.fori_loop(0, slots // TILE // group, attend, 0)

    tokens = lax.broadcasted_iota(jnp.int32, (tok_dev, slots), 0)
    for s in range(sources):
        wanted = idx_row_ref[pl.ds(index_ref[0] ^ s, 1), :]
        picks = jnp.where(tokens == wanted, 1.0, 0.0).astype(jnp.bfloat16)
        rows = dot(picks, blended[s]).astype(jnp.bfloat16)
        outs[s][:tok_dev, :] = rows
        wide = rows.astype(jnp.float32)
        squares = jnp.sum((wide * wide).T, axis=0, keepdims=True)
        lines = [squares[:, p : p + LANES] for p in range(0, tok_dev, LANES)]
        coarse = [line.astype(jnp.bfloat16).astype(jnp.float32) for line in lines]
        fine = [line - high for line, high in zip(lines, coarse)]
        spare = [jnp.zeros_like(lines[0])] * (TILE - 2 * len(lines))
        outs[s][tok_dev:, :] = jnp.concatenate(coarse + fine + spare, axis=0).astype(jnp.bfloat16)


def tables_kernel(tok_dev, segment, *refs):
    blocks, (idx_col_ref, idx_row_ref) = refs[:-2], refs[-2:]
    sources = len(blocks)
    width = sources * segment
    square = (LANES, LANES)
    row = lax.broadcasted_iota(jnp.int32, square, 0)
    lane = lax.broadcasted_iota(jnp.int32, square, 1)

    def ones_where(condition):
        return jnp.where(condition, 1.0, 0.0)

    spread = ones_where(row[:, :width] // segment == lane[:, :width]).astype(jnp.bfloat16)
    mine = (lane % segment == row % segment) & (lane < 2 * width)
    weight = jnp.where(row < width, float(DIGIT), 1.0) * ones_where(row < 2 * width)
    slot_of = row % width // segment
    columns = jnp.zeros(square, jnp.float32)
    by_row = (weight * ones_where(slot_of == lane))[:, :sources].T.astype(jnp.bfloat16)
    for r, block in enumerate(blocks):
        spread_digits = dot(spread, block[-width:, :])
        digits = jnp.where(mine, spread_digits, 0.0).astype(jnp.bfloat16)
        place = (lane // sources == slot_of) & (lane % sources == r)
        columns += dot(digits, (weight * ones_where(place)).astype(jnp.bfloat16))
        line = lax.dot_general(by_row, digits, BY_ROWS, preferred_element_type=jnp.float32)
        idx_row_ref[:, r * LANES : (r + 1) * LANES] = line.astype(jnp.int32) - tok_dev * row[:sources]
    idx_col_ref[...] = columns.astype(jnp.int32) - tok_dev * (lane // sources)


def run_tables(blocks, tok_dev, segment):
    sources = len(blocks)
    return pl.pallas_call(
        functools.partial(tables_kernel, tok_dev, segment),
        out_shape=(
            jax.ShapeDtypeStruct((LANES, LANES), jnp.int32),
            jax.ShapeDtypeStruct((sources, sources * LANES), jnp.int32),
        ),
        in_specs=[VMEM] * sources,
        out_specs=(VMEM, VMEM),
        compiler_params=pltpu.CompilerParams(vmem_limit_bytes=8 * 2**20),
        name="tables",
    )(*blocks)


def run_attention(index, after, key_blocks, pair_blocks, tables, tok_dev, segment, group=16):
    sources, head_dim = len(key_blocks), key_blocks[0].shape[1]
    idx_col, idx_row = tables
    slots = idx_row.shape[1]
    flops = 2 * sources * slots * tok_dev * head_dim
    gathered_keys = pl.pallas_call(
        gather_keys_kernel,
        out_shape=jax.ShapeDtypeStruct((sources, slots, 3 * head_dim), jnp.bfloat16),
        in_specs=[SMEM] + [VMEM] * (sources + 1),
        out_specs=VMEM,
        scratch_shapes=[pltpu.VMEM((sources, tok_dev, 3 * head_dim), jnp.bfloat16)],
        compiler_params=pltpu.CompilerParams(vmem_limit_bytes=24 * 2**20),
        cost_estimate=pl.CostEstimate(
            flops=4 * flops, bytes_accessed=6 * sources * tok_dev * head_dim, transcendentals=0
        ),
        name="gather_keys",
    )(index, *key_blocks, idx_col)
    near = sources // 2
    early = [gather_pairs(index, pair_blocks[:near], idx_col, 0, slots)] + [
        gather_pairs(index, pair_blocks[s : s + 1], idx_col, s, slots)
        for s in range(near, sources - 1)
    ]
    return pl.pallas_call(
        functools.partial(attention_kernel, segment, group, len(early)),
        out_shape=[jax.ShapeDtypeStruct((tok_dev + TILE, head_dim), jnp.bfloat16)] * sources,
        in_specs=[SMEM, pl.BlockSpec(memory_space=pl.ANY)] + [VMEM] * (len(early) + 4),
        out_specs=[VMEM] * sources,
        scratch_shapes=[
            pltpu.VMEM((1, tok_dev, 2 * head_dim), jnp.bfloat16),
            pltpu.VMEM((1, slots, 2 * head_dim), jnp.bfloat16),
            pltpu.VMEM((sources, slots, head_dim), jnp.bfloat16),
        ],
        compiler_params=pltpu.CompilerParams(vmem_limit_bytes=40 * 2**20),
        cost_estimate=pl.CostEstimate(
            flops=8 * flops,
            bytes_accessed=8 * sources * tok_dev * head_dim,
            transcendentals=slots // TILE * (sources * TILE) ** 2,
        ),
        name="attention",
    )(index, after, pair_blocks[-1], *early, gathered_keys, idx_col, idx_row)


def sum_squares_kernel(lines, *refs):
    total = sum(ref[-TILE:, :].astype(jnp.float32) for ref in refs[:-1])
    refs[-1][...] = total[:lines, :] + total[lines : 2 * lines, :]


def sum_squares(parts, tok_dev):
    lines = tok_dev // LANES
    return pl.pallas_call(
        functools.partial(sum_squares_kernel, lines),
        out_shape=jax.ShapeDtypeStruct((lines, LANES), jnp.float32),
        in_specs=[VMEM] * len(parts),
        out_specs=VMEM,
        compiler_params=pltpu.CompilerParams(vmem_limit_bytes=8 * 2**20),
        name="sum_squares",
    )(*parts)


def collect_kernel(index_ref, *refs):
    parts, (out_ref, pot_ref) = refs[:-2], refs[-2:]
    cluster_dev = out_ref.shape[1]
    for s, ref in enumerate(parts):
        head = index_ref[0] ^ s
        out_ref[head] = ref[:cluster_dev, :]
        pot_ref[pl.ds(head, 1), :] = ref[cluster_dev : cluster_dev + 1, :]


def collect(index, parts, cluster_dev):
    return pl.pallas_call(
        collect_kernel,
        out_shape=(
            jax.ShapeDtypeStruct((len(parts), cluster_dev, LANES), jnp.float32),
            jax.ShapeDtypeStruct((len(parts), LANES), jnp.float32),
        ),
        in_specs=[SMEM] + [VMEM] * len(parts),
        out_specs=(VMEM, VMEM),
        compiler_params=pltpu.CompilerParams(vmem_limit_bytes=8 * 2**20),
        name="collect",
    )(index, *parts)


def norm_kernel(width, heads, index_ref, *refs):
    parts, squares, (gain_ref, out_ref) = refs[:heads], refs[heads:-2], refs[-2:]
    head_dim = parts[0].shape[1]
    total = sum(ref[...] for ref in squares)
    inverse = lax.rsqrt(total / width + 1e-06)
    columns = [
        jnp.broadcast_to(inverse[p : p + 1, :], (LANES, LANES)).T for p in range(total.shape[0])
    ]
    for s, ref in enumerate(parts):
        head = index_ref[0] ^ s
        lanes = pl.ds(pl.multiple_of(head * head_dim, head_dim), head_dim)
        gain = gain_ref[:, lanes]
        for p, column in enumerate(columns):
            rows = slice(p * LANES, (p + 1) * LANES)
            out_ref[rows, lanes] = (ref[rows, :].astype(jnp.float32) * column * gain).astype(
                jnp.bfloat16
            )


def run_norm(index, parts, squares, gain, width, tok_dev):
    head_dim = parts[0].shape[1]
    return pl.pallas_call(
        functools.partial(norm_kernel, width, len(parts)),
        out_shape=jax.ShapeDtypeStruct((tok_dev, len(parts) * head_dim), jnp.bfloat16),
        in_specs=[SMEM] + [VMEM] * (len(parts) + len(squares) + 1),
        out_specs=VMEM,
        compiler_params=pltpu.CompilerParams(vmem_limit_bytes=24 * 2**20),
        name="norm",
    )(index, *parts, *squares, gain.reshape(1, -1))


def pack_kernel(index_ref, key_ref, centroid_ref, list_ref, count_ref, *outs):
    tok_dev = key_ref.shape[0]
    _, cluster_dev, head_dim = centroid_ref.shape
    width, sources = list_ref.shape[2], count_ref.shape[1]
    segment = width // sources
    owner = lax.broadcasted_iota(jnp.int32, (sources, width), 1) // segment
    spread = jnp.where(
        owner == lax.broadcasted_iota(jnp.int32, (sources, width), 0), 1.0, 0.0
    ).astype(jnp.bfloat16)
    slot = lax.broadcasted_iota(jnp.int32, (cluster_dev, width), 1) % segment
    at = lax.broadcasted_iota(jnp.int32, (width, head_dim), 1)
    source = lax.broadcasted_iota(jnp.int32, (width, head_dim), 0)
    first = jnp.where(at == source, 1.0, 0.0).astype(jnp.bfloat16)
    second = jnp.where(at == source + width, 1.0, 0.0).astype(jnp.bfloat16)
    for s, out in enumerate(outs):
        head = index_ref[0] ^ s
        lanes = pl.ds(pl.multiple_of(head * head_dim, head_dim), head_dim)
        out[:tok_dev, :] = key_ref[:, lanes]
        out[tok_dev : tok_dev + cluster_dev, :] = centroid_ref[head].astype(jnp.bfloat16)
        counts = lax.dot_general(
            count_ref[head].astype(jnp.float32).astype(jnp.bfloat16), spread,
            (((0,), (0,)), ((), ())), preferred_element_type=jnp.float32,
        )
        marked = jnp.where(slot.astype(jnp.float32) < counts, list_ref[head], -TILE)
        coarse = (marked >> 6).astype(jnp.float32).astype(jnp.bfloat16)
        fine = (marked & (DIGIT - 1)).astype(jnp.float32).astype(jnp.bfloat16)
        out[tok_dev + cluster_dev :, :] = (dot(coarse, first) + dot(fine, second)).astype(
            jnp.bfloat16
        )


def pack_keys(index, key_rows, centroids, cluster_lists, live_counts):
    heads, cluster_dev, head_dim = centroids.shape
    rows = key_rows.shape[0] + 2 * cluster_dev
    return pl.pallas_call(
        pack_kernel,
        out_shape=[jax.ShapeDtypeStruct((rows, head_dim), jnp.bfloat16)] * heads,
        in_specs=[SMEM] + [VMEM] * 4,
        out_specs=[VMEM] * heads,
        compiler_params=pltpu.CompilerParams(vmem_limit_bytes=60 * 2**20),
        name="pack_keys",
    )(index, key_rows, centroids, cluster_lists, live_counts.transpose(0, 2, 1))


def shift_ring(size, step):
    return [(j, (j + step) % size) for j in range(size)]


def far_first(size):
    return list(range(size // 2, size)) + list(range(1, size // 2))


def pack_kernel(index_ref, key_ref, centroid_ref, list_ref, count_ref, *outs):
    tok_dev = key_ref.shape[0]
    _, cluster_dev, head_dim = centroid_ref.shape
    width, sources = list_ref.shape[2], count_ref.shape[1]
    segment = width // sources
    owner = lax.broadcasted_iota(jnp.int32, (sources, width), 1) // segment
    spread = jnp.where(
        owner == lax.broadcasted_iota(jnp.int32, (sources, width), 0), 1.0, 0.0
    ).astype(jnp.bfloat16)
    slot = lax.broadcasted_iota(jnp.int32, (cluster_dev, width), 1) % segment
    at = lax.broadcasted_iota(jnp.int32, (width, head_dim), 1)
    source = lax.broadcasted_iota(jnp.int32, (width, head_dim), 0)
    first = jnp.where(at == source, 1.0, 0.0).astype(jnp.bfloat16)
    second = jnp.where(at == source + width, 1.0, 0.0).astype(jnp.bfloat16)
    for s, out in enumerate(outs):
        head = index_ref[0] ^ s
        lanes = pl.ds(pl.multiple_of(head * head_dim, head_dim), head_dim)
        out[:tok_dev, :] = key_ref[:, lanes]
        out[tok_dev : tok_dev + cluster_dev, :] = centroid_ref[head].astype(jnp.bfloat16)
        counts = lax.dot_general(
            count_ref[head].astype(jnp.float32).astype(jnp.bfloat16), spread,
            (((0,), (0,)), ((), ())), preferred_element_type=jnp.float32,
        )
        marked = jnp.where(slot.astype(jnp.float32) < counts, list_ref[head], -TILE)
        coarse = (marked >> 6).astype(jnp.float32).astype(jnp.bfloat16)
        fine = (marked & (DIGIT - 1)).astype(jnp.float32).astype(jnp.bfloat16)
        out[tok_dev + cluster_dev :, :] = (dot(coarse, first) + dot(fine, second)).astype(
            jnp.bfloat16
        )


def pack_keys(index, key_rows, centroids, cluster_lists, live_counts):
    heads, cluster_dev, head_dim = centroids.shape
    rows = key_rows.shape[0] + 2 * cluster_dev
    return pl.pallas_call(
        pack_kernel,
        out_shape=[jax.ShapeDtypeStruct((rows, head_dim), jnp.bfloat16)] * heads,
        in_specs=[SMEM] + [VMEM] * 4,
        out_specs=[VMEM] * heads,
        compiler_params=pltpu.CompilerParams(vmem_limit_bytes=60 * 2**20),
        name="pack_keys",
    )(index, key_rows, centroids, cluster_lists, live_counts.transpose(0, 2, 1))


def shift_ring(size, step):
    return [(j, (j + step) % size) for j in range(size)]


def exchange(blocks):
    size = len(blocks)
    arrived = list(blocks)
    for s in far_first(size):
        arrived[s] = lax.ppermute(blocks[s], "ctx", [(j, j ^ s) for j in range(size)])
    return arrived


def local(query_rows, key_rows, value_rows, centroids, norm_gain, cluster_lists, live_counts):
    context_length = lax.axis_size("ctx")
    head_dev = centroids.shape[0]
    if head_dev != context_length or context_length & (context_length - 1):
        return local_wide(
            query_rows, key_rows, value_rows, centroids, norm_gain, cluster_lists, live_counts
        )
    return local_heads(
        query_rows, key_rows, value_rows, centroids, norm_gain, cluster_lists, live_counts
    )


def local_heads(query_rows, key_rows, value_rows, centroids, norm_gain, cluster_lists, live_counts):
    context_length = lax.axis_size("ctx")
    head_size = lax.axis_size("head")
    tok_dev = query_rows.shape[0]
    head_dev, cluster_dev, head_dim = centroids.shape
    segment = cluster_lists.shape[2] // context_length
    index = lax.axis_index("ctx")
    place = index.astype(jnp.int32).reshape(1)

    def by_head(rows):
        return rows.reshape(tok_dev, head_dev, head_dim).transpose(1, 0, 2)

    pairs = jnp.concatenate([by_head(query_rows), by_head(value_rows)], axis=2)
    pairs = [
        lax.dynamic_index_in_dim(pairs, index ^ s, 0, keepdims=False)
        for s in range(context_length)
    ]
    key_blocks = exchange(pack_keys(place, key_rows, centroids, cluster_lists, live_counts))
    pair_blocks = exchange(pairs)
    tables = run_tables(key_blocks, tok_dev, segment)
    swept = run_sweeps(key_blocks, tok_dev, cluster_dev)
    outs = run_attention(place, swept[0], key_blocks, pair_blocks, tables, tok_dev, segment)
    parts = exchange(outs)
    swept_mine, potential_mine = collect(place, exchange(swept), cluster_dev)
    mine = sum_squares(parts, tok_dev)
    squares = [mine] + [
        lax.ppermute(mine, "head", shift_ring(head_size, step)) for step in range(1, head_size)
    ]
    features = head_dev * head_dim * head_size
    normalized = run_norm(place, parts, squares, norm_gain, features, tok_dev)
    return (normalized, swept_mine, potential_mine[:, :cluster_dev])


def solution(mesh):
    placed = (
        P("ctx", "head"),
        P("ctx", "head"),
        P("ctx", "head"),
        P("head", "ctx", None),
        P("head"),
        P("head", "ctx", None),
        P("head", "ctx", None),
    )
    return jax.shard_map(
        local,
        mesh=mesh,
        in_specs=placed,
        out_specs=(P("ctx", "head"), P("head", "ctx", None), P("head", "ctx")),
        check_vma=False,
    )
```
